256 devices in a mesh: src: 8 (over y, x_lo), lat: 32 (over x_hi, z, core).
Axes of the slice: x: 4 (x_hi: 2, x_lo: 2; x = x_hi * 2 + x_lo), y: 4, z: 8, core: 2. Of those that a mesh axis runs over, the one named last changes fastest.
Arguments:
- residual_rows: bfloat16 [1024, 8192], P(None, 'src'), may hold values from -6 to 6
- encoder: bfloat16 [8192, 32768], P('src', 'lat'), may hold values from -0.0625 to 0.0625
- decoder: bfloat16 [32768, 8192], P('lat', 'src'), may hold values from -0.0625 to 0.0625
- enc_bias: float32 [32768], P('lat'), may hold values from -3 to 3
- dec_bias: float32 [8192], P('src'), may hold values from -3 to 3
Outputs:
- grad_encoder: bfloat16 [8192, 32768], P('src', 'lat')
- grad_decoder: bfloat16 [32768, 8192], P('lat', 'src')
The draws below stay inside these ranges and needn't reach their ends.
All inputs are finite; a program needn't handle non-finite values.
Results may differ from the reference program's by a relative error of at most 0.024.
Values may be sent and summed in bfloat16 or wider, within the bound.
No kernel may reach another device: no remote copies, remote signals or barrier semaphores. Data moves between devices by JAX's collectives and lax.ppermute only.
A program may use at most 64 MiB of HBM per device.

```python
import math
import jax
import jax.numpy as jnp
from jax import lax

D = 4096
SRCS = 2
ROWS = 1024
FEAT = 8192
FEAT_DEV = 1024
LATENTS = 32768
N_SRC = 8


def spiked(entries, key, source, target, parts, factor):
    def block_of(dim):
        return (jnp.arange(entries.shape[dim]) // (entries.shape[dim] // parts)).reshape((-1,) + (1,) * (entries.ndim - 1 - dim))

    first = jax.random.permutation(key, parts)[block_of(target)]
    second = (block_of(target) + parts // 2) % parts
    return jnp.where((block_of(source) == first) | (block_of(source) == second), factor * entries, entries)


def level_of(key, extent, split, smallest, top_value):
    def one(axis_at, blocks):
        draws = jax.random.uniform(jax.random.fold_in(jax.random.fold_in(key, 6), axis_at), (blocks,), jnp.float32, smallest / len(split), top_value / len(split))
        return jnp.repeat(jnp.exp(draws), extent[axis_at] // blocks).reshape((-1,) + (1,) * (len(extent) - axis_at - 1))

    level = one(*split[0])
    for cut in split[1:]:
        level = level * one(*cut)
    return level


def normal_values(key, shape, deviation, most, cuts=(), held_as=jnp.bfloat16):
    entries = deviation * jax.random.normal(key, shape, jnp.float32)
    if cuts:
        entries = entries * level_of(key, shape, cuts, -0.22, 0.18)
    return jnp.clip(entries, -most, most).astype(held_as)


def heavy_noise(own_key, dims, width, bound, cuts, heavy, held_as=jnp.bfloat16):
    values = width * jax.random.normal(own_key, dims, jnp.float32)
    if cuts:
        values = values * level_of(own_key, dims, cuts, -0.22, 0.18)
    return jnp.clip(spiked(values, jax.random.fold_in(own_key, 3), *heavy), -bound, bound).astype(held_as)


def setup_inputs(seed: int = 0) -> dict:
    arg_keys = jax.random.split(jax.random.key(seed), 6)
    residual_rows = normal_values(arg_keys[0], (ROWS, FEAT), 1.0, 6.0, ((1, 8),))
    encoder = normal_values(arg_keys[1], (FEAT, LATENTS), FEAT ** -0.5, 0.0625, ((0, 8), (1, 32)))
    decoder = heavy_noise(arg_keys[2], (LATENTS, FEAT), LATENTS ** -0.5, 0.0625, ((0, 32), (1, 8)), (1, 0, 32, 2.75))
    enc_bias = normal_values(arg_keys[3], (LATENTS,), 0.5, 3.0, ((0, 32),), jnp.float32)
    dec_bias = normal_values(arg_keys[4], (FEAT,), 0.5, 3.0, ((0, 8),), jnp.float32)
    return dict(residual_rows=residual_rows, encoder=encoder, decoder=decoder, enc_bias=enc_bias, dec_bias=dec_bias)


SHARPNESS = 8.0
PENALTY = 1.0
EPSILON = 1e-06

def reference(residual_rows, encoder, decoder, enc_bias, dec_bias):
    loss_scale = 1.0 / math.sqrt(ROWS)
    pre_act = jnp.zeros((ROWS, LATENTS), jnp.float32) + enc_bias.astype(jnp.float32)[None, :]
    for block_idx in range(N_SRC):
        low = block_idx * FEAT_DEV
        partial_k = jnp.dot(residual_rows[:, low:low + FEAT_DEV], encoder[low:low + FEAT_DEV, :], preferred_element_type=jnp.float32).astype(jnp.bfloat16)
        partial_k = lax.optimization_barrier(partial_k)
        pre_act = pre_act + partial_k.astype(jnp.float32)
    latent_act = (jax.nn.softplus(SHARPNESS * pre_act) / SHARPNESS).astype(jnp.bfloat16)
    gate_slope = jax.nn.sigmoid(SHARPNESS * pre_act)
    recon = jnp.dot(latent_act, decoder, preferred_element_type=jnp.float32) + dec_bias.astype(jnp.float32)[None, :]
    errors = (recon - residual_rows.astype(jnp.float32)).astype(jnp.bfloat16)
    norm_list = []
    for source in range(SRCS):
        piece_dec = decoder[:, source * D:(source + 1) * D].astype(jnp.float32)
        norm_list.append(jnp.sqrt(lax.optimization_barrier(jnp.sum(piece_dec * piece_dec, axis=1)) + EPSILON))
    dec_norms = jnp.stack(norm_list, axis=0)
    penalty = PENALTY * lax.optimization_barrier(jnp.sum(dec_norms, axis=0))
    col_sums = lax.optimization_barrier(jnp.sum(latent_act.astype(jnp.float32), axis=0))
    outer = jnp.dot(latent_act.T, errors, preferred_element_type=jnp.float32)
    grad_list = []
    for source in range(SRCS):
        piece_dec = decoder[:, source * D:(source + 1) * D].astype(jnp.float32)
        shrink = loss_scale * PENALTY * col_sums / dec_norms[source]
        grad_list.append((loss_scale * outer[:, source * D:(source + 1) * D] + shrink[:, None] * piece_dec).astype(jnp.bfloat16))
    grad_decoder = jnp.concatenate(grad_list, axis=1)
    act_grad = jnp.zeros((ROWS, LATENTS), jnp.float32) + penalty[None, :]
    for block_idx in range(N_SRC):
        low = block_idx * FEAT_DEV
        back_k = jnp.dot(errors[:, low:low + FEAT_DEV], decoder[:, low:low + FEAT_DEV].T, preferred_element_type=jnp.float32).astype(jnp.bfloat16)
        back_k = lax.optimization_barrier(back_k)
        act_grad = act_grad + back_k.astype(jnp.float32)
    grad_pre = (loss_scale * act_grad * gate_slope).astype(jnp.bfloat16)
    grad_encoder = jnp.dot(residual_rows.T, grad_pre, preferred_element_type=jnp.float32).astype(jnp.bfloat16)
    return (grad_encoder, grad_decoder)
```

```python
import math

import jax
import jax.numpy as jnp
from jax import lax
from jax.sharding import Mesh
from jax.sharding import PartitionSpec as P

D = 4096
SRCS = 2

SHARPNESS = 8.0
PENALTY = 1.0
EPSILON = 1e-06

SRC = ("y", "xl")
LAT = ("xh", "z", "core")
RING = ("xh", "z")
CHUNKS = 2


def swap(value, axis, size, mask):
    return lax.ppermute(value, axis, [(i, i ^ mask) for i in range(size)])


def scatter_sum(partial, axes, size):
    rows = partial.shape[0] // size
    got = lax.all_to_all(partial.reshape(size, rows, -1), axes, 0, 0)
    return jnp.sum(got.astype(jnp.float32), axis=0)


def gather(shard, axes, size):
    got = lax.all_to_all(jnp.broadcast_to(shard[None], (size,) + shard.shape), axes, 0, 0)
    return got.reshape(size * shard.shape[0], -1)


def make_per_device(sizes):
    n_y, n_xl, n_xh, n_z, n_core = (sizes[a] for a in ("y", "xl", "xh", "z", "core"))
    n_src = n_y * n_xl
    n_ring = n_xh * n_z

    def per_device(residual_rows, encoder, decoder, enc_bias, dec_bias):
        row_count, feat_dev = residual_rows.shape
        loss_scale = 1.0 / math.sqrt(row_count)
        chunk = row_count // CHUNKS
        half = chunk // n_core
        core = lax.axis_index("core")
        ring = lax.axis_index(RING)

        squares = jnp.sum(jnp.square(decoder.astype(jnp.float32)), axis=1)
        own_sq = squares + swap(squares, "xl", n_xl, 1)
        own_sq = own_sq + swap(own_sq, "y", n_y, 1)
        other_sq = swap(own_sq, "y", n_y, 2)
        own_norm = jnp.sqrt(own_sq + EPSILON)
        penalty = PENALTY * (own_norm + jnp.sqrt(other_sq + EPSILON))

        chunks = [slice(i * chunk, (i + 1) * chunk) for i in range(CHUNKS)]
        latents, slopes, all_errors, grads = [], [], [], []
        for rows in chunks:
            partial = jnp.dot(
                residual_rows[rows], encoder, preferred_element_type=jnp.float32
            ).astype(jnp.bfloat16)
            pre_act = scatter_sum(partial, SRC, n_src) + enc_bias[None, :]
            latent = (jax.nn.softplus(SHARPNESS * pre_act) / SHARPNESS).astype(jnp.bfloat16)
            slopes.append(jax.nn.sigmoid(SHARPNESS * pre_act))
            latents.append(gather(latent, SRC, n_src))
        for i, rows in enumerate(chunks):
            halves = latents[i].reshape(n_core, half, -1)
            theirs = jnp.dot(
                lax.dynamic_index_in_dim(halves, 1 - core, 0, False),
                decoder,
                preferred_element_type=jnp.float32,
            ).astype(jnp.bfloat16)
            theirs = swap(theirs, "core", n_core, 1)
            mine = jnp.dot(
                lax.dynamic_index_in_dim(halves, core, 0, False),
                decoder,
                preferred_element_type=jnp.float32,
            )
            mine = (mine + theirs.astype(jnp.float32)).astype(jnp.bfloat16)
            recon = scatter_sum(mine, RING, n_ring) + dec_bias[None, :]
            own = half // n_ring
            target = lax.dynamic_slice_in_dim(
                residual_rows, rows.start + core * half + ring * own, own, 0
            )
            errors = (recon - target.astype(jnp.float32)).astype(jnp.bfloat16)
            errors = gather(errors, RING, n_ring)
            other = swap(errors, "core", n_core, 1)
            first = core == 0
            errors = jnp.concatenate(
                [jnp.where(first, errors, other), jnp.where(first, other, errors)], axis=0
            )
            all_errors.append(errors)
        for i, rows in enumerate(chunks):
            back = jnp.einsum(
                "bk,jk->bj", all_errors[i], decoder, preferred_element_type=jnp.float32
            ).astype(jnp.bfloat16)
            act_grad = scatter_sum(back, SRC, n_src)
            grad_pre = (loss_scale * (act_grad + penalty[None, :]) * slopes[i]).astype(jnp.bfloat16)
            grads.append(gather(grad_pre, SRC, n_src))
        latent_act = jnp.concatenate(latents, axis=0)
        errors = jnp.concatenate(all_errors, axis=0)
        grad_pre = jnp.concatenate(grads, axis=0)
        col_sums = jnp.sum(latent_act.astype(jnp.float32), axis=0)
        outer = jnp.einsum("bj,bk->jk", latent_act, errors, preferred_element_type=jnp.float32)
        shrink = loss_scale * PENALTY * col_sums / own_norm
        grad_decoder = (
            loss_scale * outer + shrink[:, None] * decoder.astype(jnp.float32)
        ).astype(jnp.bfloat16)
        grad_encoder = jnp.einsum(
            "bk,bj->kj", residual_rows, grad_pre, preferred_element_type=jnp.float32
        ).astype(jnp.bfloat16)
        return (grad_encoder, grad_decoder)

    return per_device


def solution(mesh):
    names = ("y", "xl", "xh", "z", "core")
    shape = (4, 2, 2, 8, 2)
    fine = Mesh(mesh.devices.reshape(shape), names)
    in_specs = (P(None, SRC), P(SRC, LAT), P(LAT, SRC), P(LAT), P(SRC))
    out_specs = (P(SRC, LAT), P(LAT, SRC))
    return jax.shard_map(
        make_per_device(dict(zip(names, shape))),
        mesh=fine,
        in_specs=in_specs,
        out_specs=out_specs,
        check_vma=False,
    )
```

```python
import math

import jax
import jax.numpy as jnp
from jax import lax
from jax.sharding import Mesh
from jax.sharding import PartitionSpec as P

D = 4096
SRCS = 2

SHARPNESS = 8.0
PENALTY = 1.0
EPSILON = 1e-06

NAMES = ("y", "xl", "xh", "z", "core")
SHAPE = (4, 2, 2, 8, 2)
N_Y, N_XL, N_XH, N_Z, N_CORE = SHAPE
SRC = ("y", "xl")
LAT = ("xh", "z", "core")
RING = ("xh", "z")
N_SRC = N_Y * N_XL
N_RING = N_XH * N_Z

NEAR = ((0, 0), (0, 1), (1, 0), (3, 0))
FAR = ((2, 0), (1, 1), (3, 1), (2, 1))

bf16 = jnp.bfloat16
f32 = jnp.float32


def swap(value, axis, size, mask):
    return lax.ppermute(value, axis, [(i, i ^ mask) for i in range(size)])


def place(offsets, slot, core):
    return offsets[(slot + 2 * core) % 4]


def behind(y, x, offset):
    return (y - offset[0]) % N_Y, x ^ offset[1]


def move(value, offsets, slot, to_owner):
    pairs = []
    for y in range(N_Y):
        for x in range(N_XL):
            for core in range(N_CORE):
                oy, ox = behind(y, x, place(offsets, slot, core))
                here = (y * N_XL + x) * N_CORE + core
                there = (oy * N_XL + ox) * N_CORE + core
                pairs.append((here, there) if to_owner else (there, here))
    return lax.ppermute(value, ("y", "xl", "core"), pairs)


def dot(a, b):
    return jnp.dot(a, b, preferred_element_type=f32)


def dot_t(a, b):
    return jnp.einsum("bk,jk->bj", a, b, preferred_element_type=f32)


def per_device(residual_rows, encoder, decoder, enc_bias, dec_bias):
    row_count = residual_rows.shape[0]
    loss_scale = 1.0 / math.sqrt(row_count)
    block = row_count // N_SRC
    y, x, core = (lax.axis_index(a) for a in ("y", "xl", "core"))
    ring = lax.axis_index(RING)
    first = core == 0

    def owner_row(offsets, slot):
        rows = []
        for c in range(N_CORE):
            oy, ox = behind(y, x, place(offsets, slot, c))
            rows.append((oy * N_XL + ox) * block)
        return jnp.where(first, rows[0], rows[1])

    def rows_of(start, count):
        return lax.dynamic_slice_in_dim(residual_rows, start, count, 0)

    own_row = (y * N_XL + x) * block

    def near_pair(offset_from):
        oy, ox = behind(y, x, NEAR[2])
        return (oy * N_XL + ox) * block

    twin = tuple(NEAR[2] for _ in range(4))
    sends = [(FAR, 3), (FAR, 1), (FAR, 2), (FAR, 0), (NEAR, 1), (NEAR, 3), (twin, 0)]

    def reduce_src(pieces):
        got = [move(p, offsets, slot, True) for p, (offsets, slot) in zip(pieces, sends)]
        return got

    def gather_src(shard):
        order = [(twin, 0), (NEAR, 1), (NEAR, 3), (FAR, 0), (FAR, 1), (FAR, 2), (FAR, 3)]
        got = [move(shard, offsets, slot, False) for offsets, slot in order]
        mate, near1, near3 = got[:3]
        near = [jnp.where(first, shard, mate), near1, jnp.where(first, mate, shard), near3]
        return near, got[3:]

    pieces = [
        dot(rows_of(owner_row(offsets, slot), block), encoder).astype(bf16)
        for offsets, slot in sends
    ]
    got = reduce_src(pieces)
    pre_act = dot(rows_of(own_row, block), encoder)

    squares = jnp.sum(jnp.square(decoder.astype(f32)), axis=1)
    own_sq = squares + swap(squares, "xl", N_XL, 1)
    own_sq = own_sq + swap(own_sq, "y", N_Y, 1)
    other_sq = swap(own_sq, "y", N_Y, 2)
    own_norm = jnp.sqrt(own_sq + EPSILON)
    penalty = PENALTY * (own_norm + jnp.sqrt(other_sq + EPSILON))

    local_rows = [rows_of(owner_row(o, s), block) for o in (NEAR, FAR) for s in range(4)]
    res_t = jnp.concatenate(local_rows, axis=0).T
    pre_act, own_norm, penalty, res_t = lax.optimization_barrier(
        (pre_act, own_norm, penalty, res_t)
    )
    pre_act = pre_act + enc_bias[None, :]
    for g in got:
        pre_act = pre_act + g.astype(f32)
    latent = (jax.nn.softplus(SHARPNESS * pre_act) / SHARPNESS).astype(bf16)
    slope = jax.nn.sigmoid(SHARPNESS * pre_act)
    near, far = gather_src(latent)

    def scatter_lat(blocks, offsets):
        theirs = dot(jnp.concatenate(blocks[2:], axis=0), decoder).astype(bf16)
        theirs = swap(theirs, "core", N_CORE, 1)
        mine = dot(jnp.concatenate(blocks[:2], axis=0), decoder) + theirs.astype(f32)
        rows = 2 * block // N_RING
        shares = mine.astype(bf16).reshape(N_RING, rows, -1)
        shares = lax.all_to_all(shares, RING, 0, 0)
        recon = jnp.sum(shares.astype(f32), axis=0) + dec_bias[None, :]
        per_block = N_RING // 2
        start = jnp.where(ring < per_block, owner_row(offsets, 0), owner_row(offsets, 1))
        target = rows_of(start + (ring % per_block) * rows, rows)
        return (recon - target.astype(f32)).astype(bf16)

    def gather_lat(errors):
        errors = jnp.broadcast_to(errors[None], (N_RING,) + errors.shape)
        mine = lax.all_to_all(errors, RING, 0, 0).reshape(2 * block, -1)
        theirs = swap(mine, "core", N_CORE, 1)
        return [mine[:block], mine[block:], theirs[:block], theirs[block:]]

    near_share = scatter_lat(near, NEAR)
    far_share = scatter_lat(far, FAR)
    far_err = gather_lat(far_share)
    near_share, _ = lax.optimization_barrier((near_share, far_err[0][:8, :128]))
    near_err = gather_lat(near_share)

    got = []
    for slot in range(4):
        got.append(move(dot_t(far_err[slot], decoder).astype(bf16), FAR, slot, True))
    sent = jnp.where(first, near_err[2], near_err[0])
    kept = jnp.where(first, near_err[0], near_err[2])
    got.append(move(dot_t(sent, decoder).astype(bf16), twin, 0, True))
    got.append(move(dot_t(near_err[1], decoder).astype(bf16), NEAR, 1, True))
    got.append(move(dot_t(near_err[3], decoder).astype(bf16), NEAR, 3, True))
    act_grad = dot_t(kept, decoder) + penalty[None, :]
    for g in got:
        act_grad = act_grad + g.astype(f32)
    grad_pre = (loss_scale * act_grad * slope).astype(bf16)
    near_grad, far_grad = gather_src(grad_pre)

    latent_act = jnp.concatenate(near + far, axis=0)
    errors = jnp.concatenate(near_err + far_err, axis=0)
    col_sums = jnp.sum(latent_act.astype(f32), axis=0)
    outer = jnp.einsum("bj,bk->jk", latent_act, errors, preferred_element_type=f32)
    shrink = loss_scale * PENALTY * col_sums / own_norm
    grad_decoder = (loss_scale * outer + shrink[:, None] * decoder.astype(f32)).astype(bf16)

    half = row_count // 2
    grad_encoder = dot(res_t[:, :half], jnp.concatenate(near_grad, axis=0))
    grad_encoder = lax.optimization_barrier(grad_encoder)
    grad_encoder = grad_encoder + dot(res_t[:, half:], jnp.concatenate(far_grad, axis=0))
    return (grad_encoder.astype(bf16), grad_decoder)


def solution(mesh):
    fine = Mesh(mesh.devices.reshape(SHAPE), NAMES)
    in_specs = (P(None, SRC), P(SRC, LAT), P(LAT, SRC), P(LAT), P(SRC))
    out_specs = (P(SRC, LAT), P(LAT, SRC))
    return jax.shard_map(
        per_device, mesh=fine, in_specs=in_specs, out_specs=out_specs, check_vma=False
    )
```

```python
import math

import jax
import jax.numpy as jnp
from jax import lax
from jax.experimental import pallas as pl
from jax.experimental.pallas import tpu as pltpu
from jax.sharding import Mesh
from jax.sharding import PartitionSpec as P

D = 4096
SRCS = 2

SHARPNESS = 8.0
PENALTY = 1.0
EPSILON = 1e-06

NAMES = ("y", "xl", "xh", "z", "core")
SHAPE = (4, 2, 2, 8, 2)
N_Y, N_XL, N_XH, N_Z, N_CORE = SHAPE
SRC = ("y", "xl")
LAT = ("xh", "z", "core")
RING = ("xh", "z")
N_SRC = N_Y * N_XL
N_RING = N_XH * N_Z

NEAR = ((0, 0), (0, 1), (1, 0), (3, 0))
FAR = ((2, 0), (1, 1), (3, 1), (2, 1))

bf16 = jnp.bfloat16
f32 = jnp.float32


def swap(value, axis, size, mask):
    return lax.ppermute(value, axis, [(i, i ^ mask) for i in range(size)])


def place(offsets, slot, core):
    return offsets[(slot + 2 * core) % 4]


def behind(y, x, offset):
    return (y - offset[0]) % N_Y, x ^ offset[1]


def move(value, offsets, slot, to_owner):
    pairs = []
    for y in range(N_Y):
        for x in range(N_XL):
            for core in range(N_CORE):
                oy, ox = behind(y, x, place(offsets, slot, core))
                here = (y * N_XL + x) * N_CORE + core
                there = (oy * N_XL + ox) * N_CORE + core
                pairs.append((here, there) if to_owner else (there, here))
    return lax.ppermute(value, ("y", "xl", "core"), pairs)


def dot(a, b):
    return jnp.dot(a, b, preferred_element_type=f32)


def dot_t(a, b):
    return jnp.einsum("bk,jk->bj", a, b, preferred_element_type=f32)


def decoder_grad(latents, errors, decoder, norms, loss_scale):
    n = len(latents)
    width, feat = decoder.shape
    tile = 256

    def kernel(*refs):
        lat, err = refs[:n], refs[n : 2 * n]
        dec_ref, norm_ref, out_ref = refs[2 * n :]
        outer = jnp.zeros((tile, feat), f32)
        sums = jnp.zeros((tile, 1), f32)
        for l_ref, e_ref in zip(lat, err):
            tall = l_ref[...].T
            outer += jnp.dot(tall, e_ref[...], preferred_element_type=f32)
            sums += jnp.sum(tall.astype(f32), axis=1, keepdims=True)
        shrink = loss_scale * PENALTY * sums / norm_ref[...].T[:, :1]
        out_ref[...] = (loss_scale * outer + shrink * dec_ref[...].astype(f32)).astype(bf16)

    block = latents[0].shape[0]
    return pl.pallas_call(
        kernel,
        grid=(width // tile,),
        in_specs=[pl.BlockSpec((block, tile), lambda i: (0, i))] * n
        + [pl.BlockSpec((block, feat), lambda i: (0, 0))] * n
        + [
            pl.BlockSpec((tile, feat), lambda i: (i, 0)),
            pl.BlockSpec((8, tile), lambda i: (0, i)),
        ],
        out_specs=pl.BlockSpec((tile, feat), lambda i: (i, 0)),
        out_shape=jax.ShapeDtypeStruct(decoder.shape, bf16),
        name="decoder_grad",
    )(*latents, *errors, decoder, norms)


def transpose(value):
    rows, cols = value.shape
    tile = 256

    def kernel(in_ref, out_ref):
        out_ref[...] = in_ref[...].T

    return pl.pallas_call(
        kernel,
        grid=(cols // tile,),
        in_specs=[pl.BlockSpec((rows, tile), lambda i: (0, i))],
        out_specs=pl.BlockSpec((tile, rows), lambda i: (i, 0)),
        out_shape=jax.ShapeDtypeStruct((cols, rows), value.dtype),
        name="transpose",
    )(value)


def per_device(residual_rows, encoder, decoder, enc_bias, dec_bias):
    row_count = residual_rows.shape[0]
    loss_scale = 1.0 / math.sqrt(row_count)
    block = row_count // N_SRC
    y, x, core = (lax.axis_index(a) for a in ("y", "xl", "core"))
    ring = lax.axis_index(RING)
    first = core == 0

    def owner_row(offsets, slot):
        rows = []
        for c in range(N_CORE):
            oy, ox = behind(y, x, place(offsets, slot, c))
            rows.append((oy * N_XL + ox) * block)
        return jnp.where(first, rows[0], rows[1])

    def rows_of(start, count):
        return lax.dynamic_slice_in_dim(residual_rows, start, count, 0)

    own_row = (y * N_XL + x) * block

    twin = (NEAR[2],) * 4

    partial = dot(residual_rows, encoder).astype(bf16).reshape(N_SRC, block, -1)
    partial = lax.all_to_all(partial, SRC, 0, 0)

    squares = jnp.sum(jnp.square(decoder.astype(f32)), axis=1)
    own_sq = squares + swap(squares, "xl", N_XL, 1)
    own_sq = own_sq + swap(own_sq, "y", N_Y, 1)
    other_sq = swap(own_sq, "y", N_Y, 2)
    own_norm = jnp.sqrt(own_sq + EPSILON)
    penalty = PENALTY * (own_norm + jnp.sqrt(other_sq + EPSILON))
    res_t = transpose(residual_rows)
    enc_bias, own_norm, penalty, res_t = lax.optimization_barrier(
        (enc_bias, own_norm, penalty, res_t)
    )

    pre_act = jnp.broadcast_to(enc_bias[None, :], partial.shape[1:])
    for i in range(N_SRC):
        pre_act = pre_act + partial[i].astype(f32)
    latent = (jax.nn.softplus(SHARPNESS * pre_act) / SHARPNESS).astype(bf16)
    slope = jax.nn.sigmoid(SHARPNESS * pre_act)

    mate = move(latent, twin, 0, False)
    near1 = move(latent, NEAR, 1, False)
    near3 = move(latent, NEAR, 3, False)
    latent_far, mate = lax.optimization_barrier((latent, mate))
    far = [move(latent_far, FAR, slot, False) for slot in range(4)]
    near = [jnp.where(first, latent, mate), near1, jnp.where(first, mate, latent), near3]

    def scatter_lat(blocks, offsets):
        theirs = dot(jnp.concatenate(blocks[2:], axis=0), decoder).astype(bf16)
        theirs = swap(theirs, "core", N_CORE, 1)
        mine = dot(jnp.concatenate(blocks[:2], axis=0), decoder) + theirs.astype(f32)
        rows = 2 * block // N_RING
        shares = mine.astype(bf16).reshape(N_RING, rows, -1)
        shares = lax.all_to_all(shares, RING, 0, 0)
        recon = jnp.sum(shares.astype(f32), axis=0) + dec_bias[None, :]
        per_block = N_RING // 2
        start = jnp.where(ring < per_block, owner_row(offsets, 0), owner_row(offsets, 1))
        target = rows_of(start + (ring % per_block) * rows, rows)
        return (recon - target.astype(f32)).astype(bf16)

    def gather_lat(errors):
        errors = jnp.broadcast_to(errors[None], (N_RING,) + errors.shape)
        mine = lax.all_to_all(errors, RING, 0, 0).reshape(2 * block, -1)
        theirs = swap(mine, "core", N_CORE, 1)
        return [mine[:block], mine[block:], theirs[:block], theirs[block:]]

    near_share = scatter_lat(near, NEAR)
    far_share = scatter_lat(far, FAR)
    far_err = gather_lat(far_share)
    near_share, _ = lax.optimization_barrier((near_share, far_err[0][:8, :128]))
    near_err = gather_lat(near_share)

    got = []
    for slot in range(4):
        got.append(move(dot_t(far_err[slot], decoder).astype(bf16), FAR, slot, True))
    sent = jnp.where(first, near_err[2], near_err[0])
    kept = jnp.where(first, near_err[0], near_err[2])
    got.append(move(dot_t(sent, decoder).astype(bf16), twin, 0, True))
    got.append(move(dot_t(near_err[1], decoder).astype(bf16), NEAR, 1, True))
    got.append(move(dot_t(near_err[3], decoder).astype(bf16), NEAR, 3, True))
    act_grad = dot_t(kept, decoder) + penalty[None, :]
    for g in got:
        act_grad = act_grad + g.astype(f32)
    grad_pre = (loss_scale * act_grad * slope).astype(bf16)
    grad_pre = jnp.broadcast_to(grad_pre[None], (N_SRC,) + grad_pre.shape)
    grad_pre = lax.all_to_all(grad_pre, SRC, 0, 0).reshape(row_count, -1)

    scale = jnp.stack([own_norm] * 8)
    grad_decoder = decoder_grad(near + far, near_err + far_err, decoder, scale, loss_scale)

    grad_encoder = dot(res_t, grad_pre).astype(bf16)
    return (grad_encoder, grad_decoder)


def solution(mesh):
    fine = Mesh(mesh.devices.reshape(SHAPE), NAMES)
    in_specs = (P(None, SRC), P(SRC, LAT), P(LAT, SRC), P(LAT), P(SRC))
    out_specs = (P(SRC, LAT), P(LAT, SRC))
    return jax.shard_map(
        per_device, mesh=fine, in_specs=in_specs, out_specs=out_specs, check_vma=False
    )
```

```python
import math

import jax
import jax.numpy as jnp
from jax import lax
from jax.experimental import pallas as pl
from jax.experimental.pallas import tpu as pltpu
from jax.sharding import Mesh
from jax.sharding import PartitionSpec as P

D = 4096
SRCS = 2

SHARPNESS = 8.0
PENALTY = 1.0
EPSILON = 1e-06

NAMES = ("y", "xl", "xh", "z", "core")
SHAPE = (4, 2, 2, 8, 2)
N_Y, N_XL, N_XH, N_Z, N_CORE = SHAPE
SRC = ("y", "xl")
LAT = ("xh", "z", "core")
RING = ("xh", "z")
N_SRC = N_Y * N_XL
N_RING = N_XH * N_Z

NEAR = ((0, 0), (0, 1), (1, 0), (3, 0))
FAR = ((2, 0), (1, 1), (3, 1), (2, 1))

bf16 = jnp.bfloat16
f32 = jnp.float32


def swap(value, axis, size, mask):
    return lax.ppermute(value, axis, [(i, i ^ mask) for i in range(size)])


def place(offsets, slot, core):
    return offsets[(slot + 2 * core) % 4]


def behind(y, x, offset):
    return (y - offset[0]) % N_Y, x ^ offset[1]


def move(value, offsets, slot, to_owner):
    pairs = []
    for y in range(N_Y):
        for x in range(N_XL):
            for core in range(N_CORE):
                oy, ox = behind(y, x, place(offsets, slot, core))
                here = (y * N_XL + x) * N_CORE + core
                there = (oy * N_XL + ox) * N_CORE + core
                pairs.append((here, there) if to_owner else (there, here))
    return lax.ppermute(value, ("y", "xl", "core"), pairs)


def dot(a, b):
    return jnp.dot(a, b, preferred_element_type=f32)


def dot_t(a, b):
    return jnp.einsum("bk,jk->bj", a, b, preferred_element_type=f32)


def decoder_grad(latents, errors, decoder, norms, loss_scale):
    n = len(latents)
    width, feat = decoder.shape
    tile = 256

    def kernel(*refs):
        lat, err = refs[:n], refs[n : 2 * n]
        dec_ref, norm_ref, out_ref = refs[2 * n :]
        outer = jnp.zeros((tile, feat), f32)
        sums = jnp.zeros((tile, 1), f32)
        for l_ref, e_ref in zip(lat, err):
            tall = l_ref[...].T
            outer += jnp.dot(tall, e_ref[...], preferred_element_type=f32)
            sums += jnp.sum(tall.astype(f32), axis=1, keepdims=True)
        shrink = loss_scale * PENALTY * sums / norm_ref[...].T[:, :1]
        out_ref[...] = (loss_scale * outer + shrink * dec_ref[...].astype(f32)).astype(bf16)

    block = latents[0].shape[0]
    return pl.pallas_call(
        kernel,
        grid=(width // tile,),
        in_specs=[pl.BlockSpec((block, tile), lambda i: (0, i))] * n
        + [pl.BlockSpec((block, feat), lambda i: (0, 0))] * n
        + [
            pl.BlockSpec((tile, feat), lambda i: (i, 0)),
            pl.BlockSpec((8, tile), lambda i: (0, i)),
        ],
        out_specs=pl.BlockSpec((tile, feat), lambda i: (i, 0)),
        out_shape=jax.ShapeDtypeStruct(decoder.shape, bf16),
        name="decoder_grad",
    )(*latents, *errors, decoder, norms)


def transpose(value):
    rows, cols = value.shape
    tile = 256

    def kernel(in_ref, out_ref):
        out_ref[...] = in_ref[...].T

    return pl.pallas_call(
        kernel,
        grid=(cols // tile,),
        in_specs=[pl.BlockSpec((rows, tile), lambda i: (0, i))],
        out_specs=pl.BlockSpec((tile, rows), lambda i: (i, 0)),
        out_shape=jax.ShapeDtypeStruct((cols, rows), value.dtype),
        name="transpose",
    )(value)


def per_device(residual_rows, encoder, decoder, enc_bias, dec_bias):
    row_count = residual_rows.shape[0]
    loss_scale = 1.0 / math.sqrt(row_count)
    block = row_count // N_SRC
    y, x, core = (lax.axis_index(a) for a in ("y", "xl", "core"))
    ring = lax.axis_index(RING)
    first = core == 0

    def owner_row(offsets, slot):
        rows = []
        for c in range(N_CORE):
            oy, ox = behind(y, x, place(offsets, slot, c))
            rows.append((oy * N_XL + ox) * block)
        return jnp.where(first, rows[0], rows[1])

    def rows_of(start, count):
        return lax.dynamic_slice_in_dim(residual_rows, start, count, 0)

    own_row = (y * N_XL + x) * block

    twin = (NEAR[2],) * 4

    partial = dot(residual_rows, encoder).astype(bf16).reshape(N_SRC, block, -1)
    partial = lax.all_to_all(partial, SRC, 0, 0)

    squares = jnp.sum(jnp.square(decoder.astype(f32)), axis=1)
    res_t = transpose(residual_rows)
    enc_bias, squares, res_t = lax.optimization_barrier((enc_bias, squares, res_t))

    pre_act = jnp.broadcast_to(enc_bias[None, :], partial.shape[1:])
    for i in range(N_SRC):
        pre_act = pre_act + partial[i].astype(f32)
    latent = (jax.nn.softplus(SHARPNESS * pre_act) / SHARPNESS).astype(bf16)
    slope = jax.nn.sigmoid(SHARPNESS * pre_act)

    mate = move(latent, twin, 0, False)
    near1 = move(latent, NEAR, 1, False)
    near3 = move(latent, NEAR, 3, False)
    latent_far, mate = lax.optimization_barrier((latent, mate))
    far = [move(latent_far, FAR, slot, False) for slot in range(4)]
    near = [jnp.where(first, latent, mate), near1, jnp.where(first, mate, latent), near3]

    def core_sum(blocks):
        theirs = dot(jnp.concatenate(blocks[2:], axis=0), decoder).astype(bf16)
        theirs = swap(theirs, "core", N_CORE, 1)
        mine = dot(jnp.concatenate(blocks[:2], axis=0), decoder) + theirs.astype(f32)
        return mine.astype(bf16)

    rows = 4 * block // N_RING
    shares = jnp.concatenate([core_sum(near), core_sum(far)], axis=0)
    squares, shares = lax.optimization_barrier((squares, shares))
    shares = lax.all_to_all(shares.reshape(N_RING, rows, -1), RING, 0, 0)

    own_sq = squares + swap(squares, "xl", N_XL, 1)
    own_sq = own_sq + swap(own_sq, "y", N_Y, 1)
    other_sq = swap(own_sq, "y", N_Y, 2)
    own_norm = jnp.sqrt(own_sq + EPSILON)
    penalty = PENALTY * (own_norm + jnp.sqrt(other_sq + EPSILON))
    dec_bias, own_norm, penalty = lax.optimization_barrier((dec_bias, own_norm, penalty))

    recon = jnp.broadcast_to(dec_bias[None, :], shares.shape[1:])
    for i in range(N_RING):
        recon = recon + shares[i].astype(f32)
    per_block = N_RING // 4
    starts = jnp.stack([owner_row(o, slot) for o in (NEAR, FAR) for slot in range(2)])
    start = lax.dynamic_index_in_dim(starts, ring // per_block, 0, False)
    target = rows_of(start + (ring % per_block) * rows, rows)
    errors = (recon - target.astype(f32)).astype(bf16)
    errors = jnp.broadcast_to(errors[None], (N_RING,) + errors.shape)
    mine = lax.all_to_all(errors, RING, 0, 0).reshape(4, block, -1)
    theirs = swap(mine, "core", N_CORE, 1)
    near_err = [mine[0], mine[1], theirs[0], theirs[1]]
    far_err = [mine[2], mine[3], theirs[2], theirs[3]]

    got = []
    for slot in range(2):
        got.append(move(dot_t(far_err[slot], decoder).astype(bf16), FAR, slot, True))
    got.append(move(dot_t(near_err[1], decoder).astype(bf16), NEAR, 1, True))
    for slot in range(2, 4):
        got.append(move(dot_t(far_err[slot], decoder).astype(bf16), FAR, slot, True))
    got.append(move(dot_t(near_err[3], decoder).astype(bf16), NEAR, 3, True))
    sent = jnp.where(first, near_err[2], near_err[0])
    kept = jnp.where(first, near_err[0], near_err[2])
    got.append(move(dot_t(sent, decoder).astype(bf16), twin, 0, True))
    act_grad = dot_t(kept, decoder) + penalty[None, :]
    for g in got:
        act_grad = act_grad + g.astype(f32)
    grad_pre = (loss_scale * act_grad * slope).astype(bf16)
    grad_pre = jnp.broadcast_to(grad_pre[None], (N_SRC,) + grad_pre.shape)
    grad_pre = lax.all_to_all(grad_pre, SRC, 0, 0).reshape(row_count, -1)

    scale = jnp.stack([own_norm] * 8)
    grad_decoder = decoder_grad(near + far, near_err + far_err, decoder, scale, loss_scale)

    grad_encoder = dot(res_t, grad_pre).astype(bf16)
    return (grad_encoder, grad_decoder)


def solution(mesh):
    fine = Mesh(mesh.devices.reshape(SHAPE), NAMES)
    in_specs = (P(None, SRC), P(SRC, LAT), P(LAT, SRC), P(LAT), P(SRC))
    out_specs = (P(SRC, LAT), P(LAT, SRC))
    return jax.shard_map(
        per_device, mesh=fine, in_specs=in_specs, out_specs=out_specs, check_vma=False
    )
```

```python
import math

import jax
import jax.numpy as jnp
from jax import lax
from jax.experimental import pallas as pl
from jax.sharding import Mesh
from jax.sharding import PartitionSpec as P

SHARPNESS = 8.0
PENALTY = 1.0
EPSILON = 1e-06

NAMES = ("y", "xl", "xh", "z", "core")
SHAPE = (4, 2, 2, 8, 2)
N_Y, N_XL, N_XH, N_Z, N_CORE = SHAPE
SRC = ("y", "xl")
LAT = ("xh", "z", "core")

bf16 = jnp.bfloat16
f32 = jnp.float32


def swap(value, axis, size, mask=1):
    return lax.ppermute(value, axis, [(i, i ^ mask) for i in range(size)])


def exchange(value, axis, size):
    return lax.all_to_all(value.reshape(size, value.shape[0] // size, -1), axis, 0, 0)


def spread(value, axis, size):
    copies = jnp.broadcast_to(value[None], (size,) + value.shape)
    return lax.all_to_all(copies, axis, 0, 0).reshape(size * value.shape[0], -1)


def add_up(parts):
    total = parts[0].astype(f32)
    for i in range(1, parts.shape[0]):
        total = total + parts[i].astype(f32)
    return total


def half_of(value, index):
    return lax.dynamic_index_in_dim(
        value.reshape(2, value.shape[0] // 2, -1), index, 0, False
    )


def in_order(index, own, other):
    first = index == 0
    return jnp.concatenate(
        [jnp.where(first, own, other), jnp.where(first, other, own)], axis=0
    )


def dot(a, b):
    return jnp.dot(a, b, preferred_element_type=f32)


def dot_t(a, b):
    return jnp.einsum("bk,jk->bj", a, b, preferred_element_type=f32)


def transpose(value):
    rows, cols = value.shape
    tile = 256

    def kernel(in_ref, out_ref):
        out_ref[...] = in_ref[...].T

    return pl.pallas_call(
        kernel,
        grid=(cols // tile,),
        in_specs=[pl.BlockSpec((rows, tile), lambda i: (0, i))],
        out_specs=pl.BlockSpec((tile, rows), lambda i: (i, 0)),
        out_shape=jax.ShapeDtypeStruct((cols, rows), value.dtype),
        name="transpose",
    )(value)


def decoder_grad(latents, errors, decoder, norms, loss_scale):
    n = len(latents)
    width, feat = decoder.shape
    tile = 256

    def kernel(*refs):
        lat, err = refs[:n], refs[n : 2 * n]
        dec_ref, norm_ref, out_ref = refs[2 * n :]
        outer = jnp.zeros((tile, feat), f32)
        sums = jnp.zeros((tile, 1), f32)
        for l_ref, e_ref in zip(lat, err):
            tall = l_ref[...].T
            outer += jnp.dot(tall, e_ref[...], preferred_element_type=f32)
            sums += jnp.sum(tall.astype(f32), axis=1, keepdims=True)
        shrink = loss_scale * PENALTY * sums / norm_ref[...].T[:, :1]
        out_ref[...] = (loss_scale * outer + shrink * dec_ref[...].astype(f32)).astype(bf16)

    return pl.pallas_call(
        kernel,
        grid=(width // tile,),
        in_specs=[pl.BlockSpec((v.shape[0], tile), lambda i: (0, i)) for v in latents]
        + [pl.BlockSpec((v.shape[0], feat), lambda i: (0, 0)) for v in errors]
        + [
            pl.BlockSpec((tile, feat), lambda i: (i, 0)),
            pl.BlockSpec((8, tile), lambda i: (0, i)),
        ],
        out_specs=pl.BlockSpec((tile, feat), lambda i: (i, 0)),
        out_shape=jax.ShapeDtypeStruct(decoder.shape, bf16),
        name="decoder_grad",
    )(*latents, *errors, decoder, norms)


def encoder_grad(res_t, grads):
    n = len(grads)
    feat, rows = res_t.shape
    width = grads[0].shape[1]
    tile = 256

    def kernel(res_ref, *refs):
        total = jnp.zeros((tile, width), f32)
        low = 0
        for g_ref in refs[:n]:
            high = low + g_ref.shape[0]
            total += jnp.dot(res_ref[:, low:high], g_ref[...], preferred_element_type=f32)
            low = high
        refs[n][...] = total.astype(bf16)

    return pl.pallas_call(
        kernel,
        grid=(feat // tile,),
        in_specs=[pl.BlockSpec((tile, rows), lambda i: (i, 0))]
        + [pl.BlockSpec(g.shape, lambda i: (0, 0)) for g in grads],
        out_specs=pl.BlockSpec((tile, width), lambda i: (i, 0)),
        out_shape=jax.ShapeDtypeStruct((feat, width), bf16),
        name="encoder_grad",
    )(res_t, *grads)


def scatter_src(a_part, b_send, b_keep, x):
    a_parts = exchange(a_part, "y", N_Y)
    b_sum = (b_keep + swap(b_send, "xl", N_XL).astype(f32)).astype(bf16)
    a_sum = add_up(a_parts)
    a_got = swap(half_of(a_sum, 1 - x).astype(bf16), "xl", N_XL)
    b_total = add_up(exchange(b_sum, "y", N_Y))
    a_total = half_of(a_sum, x) + a_got.astype(f32)
    return jnp.concatenate([a_total, b_total], axis=0)


def gather_src(shard, x):
    half = shard.shape[0] // 2
    a_own, b_own = shard[:half], shard[half:]
    pair = in_order(x, a_own, swap(a_own, "xl", N_XL))
    b_near = spread(b_own, "y", N_Y)
    pair, b_near = lax.optimization_barrier((pair, b_near))
    b_far = swap(b_near, "xl", N_XL)
    return spread(pair, "y", N_Y), b_near, b_far


def per_device(residual_rows, encoder, decoder, enc_bias, dec_bias):
    row_count = residual_rows.shape[0]
    loss_scale = 1.0 / math.sqrt(row_count)
    half = row_count // 2
    quarter = half // 2
    y, x, xh, z, core = (lax.axis_index(a) for a in NAMES)

    def rows_of(start, count):
        return lax.dynamic_slice_in_dim(residual_rows, start, count, 0)

    b_near_rows = half + x * quarter
    b_far_rows = half + (1 - x) * quarter

    a_part = dot(residual_rows[:half], encoder).astype(bf16)
    b_send = dot(rows_of(b_far_rows, quarter), encoder).astype(bf16)
    b_keep = dot(rows_of(b_near_rows, quarter), encoder)
    pre_act = scatter_src(a_part, b_send, b_keep, x)

    squares = jnp.sum(jnp.square(decoder.astype(f32)), axis=1)
    res_t = transpose(
        jnp.concatenate(
            [residual_rows[:half], rows_of(b_near_rows, quarter), rows_of(b_far_rows, quarter)],
            axis=0,
        )
    )
    enc_bias, squares, res_t = lax.optimization_barrier((enc_bias, squares, res_t))

    pre_act = pre_act + enc_bias[None, :]
    latent = (jax.nn.softplus(SHARPNESS * pre_act) / SHARPNESS).astype(bf16)
    slope = jax.nn.sigmoid(SHARPNESS * pre_act)
    lat_a, lat_near, lat_far = gather_src(latent, x)

    def core_sum(mine, theirs):
        theirs = swap(dot(theirs, decoder).astype(bf16), "core", N_CORE)
        return dot(mine, decoder) + theirs.astype(f32)

    same = core == x
    b_mine = jnp.where(same, lat_near, lat_far)
    b_theirs = jnp.where(same, lat_far, lat_near)
    b_sum = core_sum(b_mine, b_theirs)
    a_sum = core_sum(half_of(lat_a, core), half_of(lat_a, 1 - core)).astype(bf16)
    squares, a_sum = lax.optimization_barrier((squares, a_sum))

    a_sum = add_up(exchange(a_sum, "z", N_Z))
    b_got = swap(half_of(b_sum, 1 - xh).astype(bf16), "xh", N_XH)
    b_sum = (half_of(b_sum, xh) + b_got.astype(f32)).astype(bf16)
    a_got = swap(half_of(a_sum, 1 - xh).astype(bf16), "xh", N_XH)
    b_sum = add_up(exchange(b_sum, "z", N_Z))
    a_sum = half_of(a_sum, xh) + a_got.astype(f32)

    own_sq = squares + swap(squares, "xl", N_XL)
    own_sq = own_sq + swap(own_sq, "y", N_Y)
    other_sq = swap(own_sq, "y", N_Y, 2)
    own_norm = jnp.sqrt(own_sq + EPSILON)
    penalty = PENALTY * (own_norm + jnp.sqrt(other_sq + EPSILON))
    dec_bias, own_norm, penalty = lax.optimization_barrier((dec_bias, own_norm, penalty))

    share = quarter // (N_XH * N_Z)
    a_target = rows_of(core * quarter + (z * N_XH + xh) * share, share)
    b_target = rows_of(half + core * quarter + (xh * N_Z + z) * share, share)
    a_err = (a_sum + dec_bias[None, :] - a_target.astype(f32)).astype(bf16)
    b_err = (b_sum + dec_bias[None, :] - b_target.astype(f32)).astype(bf16)

    a_pair = in_order(xh, a_err, swap(a_err, "xh", N_XH))
    b_err = spread(b_err, "z", N_Z)
    a_pair, b_err = lax.optimization_barrier((a_pair, b_err))
    b_mine = in_order(xh, b_err, swap(b_err, "xh", N_XH))
    a_mine = spread(a_pair, "z", N_Z)
    b_theirs = swap(b_mine, "core", N_CORE)
    err_near = jnp.where(same, b_mine, b_theirs)
    err_far = jnp.where(same, b_theirs, b_mine)
    err_a = in_order(core, a_mine, swap(a_mine, "core", N_CORE))

    b_send = dot_t(err_far, decoder).astype(bf16)
    b_keep = dot_t(err_near, decoder)
    a_part = dot_t(err_a, decoder).astype(bf16)
    act_grad = scatter_src(a_part, b_send, b_keep, x) + penalty[None, :]
    grad_pre = (loss_scale * act_grad * slope).astype(bf16)
    grads = gather_src(grad_pre, x)

    grad_decoder = decoder_grad(
        [lat_a, lat_near, lat_far],
        [err_a, err_near, err_far],
        decoder,
        jnp.stack([own_norm] * 8),
        loss_scale,
    )
    return (encoder_grad(res_t, grads), grad_decoder)


def solution(mesh):
    fine = Mesh(mesh.devices.reshape(SHAPE), NAMES)
    in_specs = (P(None, SRC), P(SRC, LAT), P(LAT, SRC), P(LAT), P(SRC))
    out_specs = (P(SRC, LAT), P(LAT, SRC))
    return jax.shard_map(
        per_device, mesh=fine, in_specs=in_specs, out_specs=out_specs, check_vma=False
    )
```

```python
import math

import jax
import jax.numpy as jnp
from jax import lax
from jax.experimental import pallas as pl
from jax.experimental.pallas import tpu as pltpu
from jax.sharding import Mesh
from jax.sharding import PartitionSpec as P

D = 4096
SRCS = 2

SHARPNESS = 8.0
PENALTY = 1.0
EPSILON = 1e-06

NAMES = ("y", "xl", "xh", "z", "core")
SHAPE = (4, 2, 2, 8, 2)
N_Y, N_XL, N_XH, N_Z, N_CORE = SHAPE
SRC = ("y", "xl")
LAT = ("xh", "z", "core")
RING = ("xh", "z")
N_SRC = N_Y * N_XL
N_RING = N_XH * N_Z

NEAR = ((0, 0), (0, 1), (1, 0), (3, 0))
FAR = ((2, 0), (1, 1), (3, 1), (2, 1))

bf16 = jnp.bfloat16
f32 = jnp.float32


def swap(value, axis, size, mask):
    return lax.ppermute(value, axis, [(i, i ^ mask) for i in range(size)])


def place(offsets, slot, core):
    return offsets[(slot + 2 * core) % 4]


def behind(y, x, offset):
    return (y - offset[0]) % N_Y, x ^ offset[1]


def move(value, offsets, slot, to_owner):
    pairs = []
    for y in range(N_Y):
        for x in range(N_XL):
            for core in range(N_CORE):
                oy, ox = behind(y, x, place(offsets, slot, core))
                here = (y * N_XL + x) * N_CORE + core
                there = (oy * N_XL + ox) * N_CORE + core
                pairs.append((here, there) if to_owner else (there, here))
    return lax.ppermute(value, ("y", "xl", "core"), pairs)


def dot(a, b):
    return jnp.dot(a, b, preferred_element_type=f32)


def dot_t(a, b):
    return jnp.einsum("bk,jk->bj", a, b, preferred_element_type=f32)


def decoder_grad(latents, errors, decoder, norms, loss_scale):
    n = len(latents)
    width, feat = decoder.shape
    tile = 256

    def kernel(*refs):
        lat, err = refs[:n], refs[n : 2 * n]
        dec_ref, norm_ref, out_ref = refs[2 * n :]
        outer = jnp.zeros((tile, feat), f32)
        sums = jnp.zeros((tile, 1), f32)
        for l_ref, e_ref in zip(lat, err):
            tall = l_ref[...].T
            outer += jnp.dot(tall, e_ref[...], preferred_element_type=f32)
            sums += jnp.sum(tall.astype(f32), axis=1, keepdims=True)
        shrink = loss_scale * PENALTY * sums / norm_ref[...].T[:, :1]
        out_ref[...] = (loss_scale * outer + shrink * dec_ref[...].astype(f32)).astype(bf16)

    block = latents[0].shape[0]
    return pl.pallas_call(
        kernel,
        grid=(width // tile,),
        in_specs=[pl.BlockSpec((block, tile), lambda i: (0, i))] * n
        + [pl.BlockSpec((block, feat), lambda i: (0, 0))] * n
        + [
            pl.BlockSpec((tile, feat), lambda i: (i, 0)),
            pl.BlockSpec((8, tile), lambda i: (0, i)),
        ],
        out_specs=pl.BlockSpec((tile, feat), lambda i: (i, 0)),
        out_shape=jax.ShapeDtypeStruct(decoder.shape, bf16),
        name="decoder_grad",
    )(*latents, *errors, decoder, norms)


def transpose(value, order, block):
    rows, cols = value.shape

    def kernel(order_ref, in_ref, out_ref):
        out_ref[...] = in_ref[...].T

    return pl.pallas_call(
        kernel,
        grid_spec=pltpu.PrefetchScalarGridSpec(
            num_scalar_prefetch=1,
            grid=(rows // block,),
            in_specs=[pl.BlockSpec((block, cols), lambda i, order_ref: (order_ref[i], 0))],
            out_specs=pl.BlockSpec((cols, block), lambda i, order_ref: (0, i)),
        ),
        out_shape=jax.ShapeDtypeStruct((cols, rows), value.dtype),
        name="transpose",
    )(order, value)


def encoder_grad(res_t, grads, part, so_far):
    n = len(grads)
    feat = res_t.shape[0]
    block, width = grads[0].shape
    tile = 256
    last = so_far is not None

    def kernel(res_ref, *refs):
        total = refs[n][...] if last else jnp.zeros((tile, width), f32)
        for i in range(n):
            total += jnp.dot(
                res_ref[:, i * block : (i + 1) * block],
                refs[i][...],
                preferred_element_type=f32,
            )
        refs[-1][...] = total.astype(refs[-1].dtype)

    spec = pl.BlockSpec((tile, width), lambda i: (i, 0))
    return pl.pallas_call(
        kernel,
        grid=(feat // tile,),
        in_specs=[pl.BlockSpec((tile, n * block), lambda i: (i, part))]
        + [pl.BlockSpec((block, width), lambda i: (0, 0))] * n
        + [spec] * last,
        out_specs=spec,
        out_shape=jax.ShapeDtypeStruct((feat, width), bf16 if last else f32),
        name="encoder_grad",
    )(res_t, *grads, *([so_far] if last else []))


def per_device(residual_rows, encoder, decoder, enc_bias, dec_bias):
    row_count = residual_rows.shape[0]
    loss_scale = 1.0 / math.sqrt(row_count)
    block = row_count // N_SRC
    y, x, core = (lax.axis_index(a) for a in ("y", "xl", "core"))
    ring = lax.axis_index(RING)
    first = core == 0

    def owner_row(offsets, slot):
        rows = []
        for c in range(N_CORE):
            oy, ox = behind(y, x, place(offsets, slot, c))
            rows.append((oy * N_XL + ox) * block)
        return jnp.where(first, rows[0], rows[1])

    def rows_of(start, count):
        return lax.dynamic_slice_in_dim(residual_rows, start, count, 0)

    own_row = (y * N_XL + x) * block

    twin = (NEAR[2],) * 4

    def gather_src(shard):
        far = [move(shard, FAR, slot, False) for slot in (3, 2, 1, 0)][::-1]
        near3, near1 = (move(shard, NEAR, slot, False) for slot in (3, 1))
        mate = move(shard, twin, 0, False)
        near = [jnp.where(first, shard, mate), near1, jnp.where(first, mate, shard), near3]
        return near, far

    partial = dot(residual_rows, encoder).astype(bf16).reshape(N_SRC, block, -1)
    partial = lax.all_to_all(partial, SRC, 0, 0)

    squares = jnp.sum(jnp.square(decoder.astype(f32)), axis=1)
    order = [owner_row(o, s) // block for o in (NEAR, FAR) for s in range(4)]
    res_t = transpose(residual_rows, jnp.stack(order), block)
    enc_bias, squares, res_t = lax.optimization_barrier((enc_bias, squares, res_t))

    pre_act = jnp.broadcast_to(enc_bias[None, :], partial.shape[1:])
    for i in range(N_SRC):
        pre_act = pre_act + partial[i].astype(f32)
    latent = (jax.nn.softplus(SHARPNESS * pre_act) / SHARPNESS).astype(bf16)
    slope = jax.nn.sigmoid(SHARPNESS * pre_act)

    near, far = gather_src(latent)

    def core_sum(blocks):
        theirs = dot(jnp.concatenate(blocks[2:], axis=0), decoder).astype(bf16)
        theirs = swap(theirs, "core", N_CORE, 1)
        mine = dot(jnp.concatenate(blocks[:2], axis=0), decoder) + theirs.astype(f32)
        return mine.astype(bf16)

    rows = 4 * block // N_RING
    shares = jnp.concatenate([core_sum(near), core_sum(far)], axis=0)
    squares, shares = lax.optimization_barrier((squares, shares))
    shares = lax.all_to_all(shares.reshape(N_RING, rows, -1), RING, 0, 0)

    own_sq = squares + swap(squares, "xl", N_XL, 1)
    own_sq = own_sq + swap(own_sq, "y", N_Y, 1)
    other_sq = swap(own_sq, "y", N_Y, 2)
    own_norm = jnp.sqrt(own_sq + EPSILON)
    penalty = PENALTY * (own_norm + jnp.sqrt(other_sq + EPSILON))
    dec_bias, own_norm, penalty = lax.optimization_barrier((dec_bias, own_norm, penalty))

    recon = jnp.broadcast_to(dec_bias[None, :], shares.shape[1:])
    for i in range(N_RING):
        recon = recon + shares[i].astype(f32)
    per_block = N_RING // 4
    starts = jnp.stack([owner_row(o, slot) for o in (NEAR, FAR) for slot in range(2)])
    start = lax.dynamic_index_in_dim(starts, ring // per_block, 0, False)
    target = rows_of(start + (ring % per_block) * rows, rows)
    errors = (recon - target.astype(f32)).astype(bf16)
    errors = jnp.broadcast_to(errors[None], (N_RING,) + errors.shape)
    mine = lax.all_to_all(errors, RING, 0, 0).reshape(4, block, -1)
    theirs = swap(mine, "core", N_CORE, 1)
    near_err = [mine[0], mine[1], theirs[0], theirs[1]]
    far_err = [mine[2], mine[3], theirs[2], theirs[3]]

    got = []
    for slot in range(2):
        got.append(move(dot_t(far_err[slot], decoder).astype(bf16), FAR, slot, True))
    got.append(move(dot_t(near_err[1], decoder).astype(bf16), NEAR, 1, True))
    for slot in range(2, 4):
        got.append(move(dot_t(far_err[slot], decoder).astype(bf16), FAR, slot, True))
    got.append(move(dot_t(near_err[3], decoder).astype(bf16), NEAR, 3, True))
    sent = jnp.where(first, near_err[2], near_err[0])
    kept = jnp.where(first, near_err[0], near_err[2])
    got.append(move(dot_t(sent, decoder).astype(bf16), twin, 0, True))
    act_grad = dot_t(kept, decoder) + penalty[None, :]
    for g in got:
        act_grad = act_grad + g.astype(f32)
    grad_pre = (loss_scale * act_grad * slope).astype(bf16)
    near_grad, far_grad = gather_src(grad_pre)

    scale = jnp.stack([own_norm] * 8)
    grad_decoder = decoder_grad(near + far, near_err + far_err, decoder, scale, loss_scale)

    grad_encoder = encoder_grad(res_t, near_grad, 0, None)
    grad_encoder = encoder_grad(res_t, far_grad, 1, grad_encoder)
    return (grad_encoder, grad_decoder)


def solution(mesh):
    fine = Mesh(mesh.devices.reshape(SHAPE), NAMES)
    in_specs = (P(None, SRC), P(SRC, LAT), P(LAT, SRC), P(LAT), P(SRC))
    out_specs = (P(SRC, LAT), P(LAT, SRC))
    return jax.shard_map(
        per_device, mesh=fine, in_specs=in_specs, out_specs=out_specs, check_vma=False
    )
```

```python
import math

import jax
import jax.numpy as jnp
from jax import lax
from jax.experimental import pallas as pl
from jax.experimental.pallas import tpu as pltpu
from jax.sharding import Mesh
from jax.sharding import PartitionSpec as P

D = 4096
SRCS = 2

SHARPNESS = 8.0
PENALTY = 1.0
EPSILON = 1e-06

NAMES = ("y", "xl", "xh", "z", "core")
SHAPE = (4, 2, 2, 8, 2)
N_Y, N_XL, N_XH, N_Z, N_CORE = SHAPE
SRC = ("y", "xl")
LAT = ("xh", "z", "core")
RING = ("xh", "z")
N_SRC = N_Y * N_XL
N_RING = N_XH * N_Z

NEAR = ((0, 0), (0, 1), (1, 0), (3, 0))
FAR = ((2, 0), (1, 1), (3, 1), (2, 1))

bf16 = jnp.bfloat16
f32 = jnp.float32


def swap(value, axis, size, mask):
    return lax.ppermute(value, axis, [(i, i ^ mask) for i in range(size)])


def place(offsets, slot, core):
    return offsets[(slot + 2 * core) % 4]


def behind(y, x, offset):
    return (y - offset[0]) % N_Y, x ^ offset[1]


def move(value, offsets, slot, to_owner):
    pairs = []
    for y in range(N_Y):
        for x in range(N_XL):
            for core in range(N_CORE):
                oy, ox = behind(y, x, place(offsets, slot, core))
                here = (y * N_XL + x) * N_CORE + core
                there = (oy * N_XL + ox) * N_CORE + core
                pairs.append((here, there) if to_owner else (there, here))
    return lax.ppermute(value, ("y", "xl", "core"), pairs)


def dot(a, b):
    return jnp.dot(a, b, preferred_element_type=f32)


def dot_t(a, b):
    return jnp.einsum("bk,jk->bj", a, b, preferred_element_type=f32)


def blocks_dot(weight, contract, dtypes, blocks=None, source=None, order=None):
    n = len(dtypes)
    tile = 256
    depth = weight.shape[contract]
    width = weight.shape[1 - contract]
    block = blocks[0].shape[0] if source is None else source.shape[0] // N_SRC

    def kernel(order_ref, *refs):
        ins, w_ref, outs, all_ref = refs[:n], refs[n], refs[n + 1 : 2 * n + 1], refs[-1]

        @pl.when(pl.program_id(0) == 0)
        def _():
            for i in range(n):
                all_ref[i * block : (i + 1) * block] = ins[i][...]

        product = lax.dot_general(
            all_ref[...], w_ref[...], (((1,), (contract,)), ((), ())), preferred_element_type=f32
        )
        for i in range(n):
            outs[i][...] = product[i * block : (i + 1) * block].astype(outs[i].dtype)

    if source is None:
        order = jnp.zeros((1,), jnp.int32)
        in_specs = [pl.BlockSpec((block, depth), lambda i, o: (0, 0))] * n
    else:
        blocks = [source] * n
        in_specs = [pl.BlockSpec((block, depth), lambda i, o, p=p: (o[p], 0)) for p in range(n)]
    if contract == 0:
        w_spec = pl.BlockSpec((depth, tile), lambda i, o: (0, i))
    else:
        w_spec = pl.BlockSpec((tile, depth), lambda i, o: (i, 0))
    return pl.pallas_call(
        kernel,
        grid_spec=pltpu.PrefetchScalarGridSpec(
            num_scalar_prefetch=1,
            grid=(width // tile,),
            in_specs=in_specs + [w_spec],
            out_specs=[pl.BlockSpec((block, tile), lambda i, o: (0, i))] * n,
            scratch_shapes=[pltpu.VMEM((n * block, depth), bf16)],
        ),
        out_shape=[jax.ShapeDtypeStruct((block, width), d) for d in dtypes],
        name="blocks_dot",
    )(order, *blocks, weight)


def decoder_grad(latents, errors, decoder, norms, loss_scale):
    n = len(latents)
    width, feat = decoder.shape
    block = latents[0].shape[0]
    rows = n * block
    tile = 256

    def kernel(*refs):
        lat, err = refs[:n], refs[n : 2 * n]
        dec_ref, norm_ref, out_ref, err_all = refs[2 * n :]

        @pl.when(pl.program_id(0) == 0)
        def _():
            for i in range(n):
                err_all[i * block : (i + 1) * block] = err[i][...]

        tall = jnp.concatenate([l_ref[...] for l_ref in lat], axis=0).T
        outer = jnp.dot(tall, err_all[...], preferred_element_type=f32)
        ones = jnp.ones((rows, 128), bf16)
        sums = jnp.dot(tall, ones, preferred_element_type=f32)[:, :1]
        shrink = loss_scale * PENALTY * sums / norm_ref[...].T[:, :1]
        out_ref[...] = (loss_scale * outer + shrink * dec_ref[...].astype(f32)).astype(bf16)

    return pl.pallas_call(
        kernel,
        grid=(width // tile,),
        in_specs=[pl.BlockSpec((block, tile), lambda i: (0, i))] * n
        + [pl.BlockSpec((block, feat), lambda i: (0, 0))] * n
        + [
            pl.BlockSpec((tile, feat), lambda i: (i, 0)),
            pl.BlockSpec((8, tile), lambda i: (0, i)),
        ],
        out_specs=pl.BlockSpec((tile, feat), lambda i: (i, 0)),
        out_shape=jax.ShapeDtypeStruct(decoder.shape, bf16),
        scratch_shapes=[pltpu.VMEM((rows, feat), bf16)],
        name="decoder_grad",
    )(*latents, *errors, decoder, norms)


def transpose(value, order, block):
    rows, cols = value.shape

    def kernel(order_ref, in_ref, out_ref):
        out_ref[...] = in_ref[...].T

    return pl.pallas_call(
        kernel,
        grid_spec=pltpu.PrefetchScalarGridSpec(
            num_scalar_prefetch=1,
            grid=(rows // block,),
            in_specs=[pl.BlockSpec((block, cols), lambda i, order_ref: (order_ref[i], 0))],
            out_specs=pl.BlockSpec((cols, block), lambda i, order_ref: (0, i)),
        ),
        out_shape=jax.ShapeDtypeStruct((cols, rows), value.dtype),
        name="transpose",
    )(order, value)


def encoder_grad(res_t, grads, part, so_far):
    n = len(grads)
    feat = res_t.shape[0]
    block, width = grads[0].shape
    tile = 256
    last = so_far is not None

    def kernel(res_ref, *refs):
        out_ref, grad_all = refs[-2:]

        @pl.when(pl.program_id(0) == 0)
        def _():
            for i in range(n):
                grad_all[i * block : (i + 1) * block] = refs[i][...]

        total = jnp.dot(res_ref[...], grad_all[...], preferred_element_type=f32)
        if last:
            total += refs[n][...]
        out_ref[...] = total.astype(out_ref.dtype)

    spec = pl.BlockSpec((tile, width), lambda i: (i, 0))
    return pl.pallas_call(
        kernel,
        grid=(feat // tile,),
        in_specs=[pl.BlockSpec((tile, n * block), lambda i: (i, part))]
        + [pl.BlockSpec((block, width), lambda i: (0, 0))] * n
        + [spec] * last,
        out_specs=spec,
        out_shape=jax.ShapeDtypeStruct((feat, width), bf16 if last else f32),
        scratch_shapes=[pltpu.VMEM((n * block, width), bf16)],
        name="encoder_grad",
    )(res_t, *grads, *([so_far] if last else []))


def per_device(residual_rows, encoder, decoder, enc_bias, dec_bias):
    row_count = residual_rows.shape[0]
    loss_scale = 1.0 / math.sqrt(row_count)
    block = row_count // N_SRC
    y, x, core = (lax.axis_index(a) for a in ("y", "xl", "core"))
    ring = lax.axis_index(RING)
    first = core == 0

    def owner_row(offsets, slot):
        rows = []
        for c in range(N_CORE):
            oy, ox = behind(y, x, place(offsets, slot, c))
            rows.append((oy * N_XL + ox) * block)
        return jnp.where(first, rows[0], rows[1])

    def rows_of(start, count):
        return lax.dynamic_slice_in_dim(residual_rows, start, count, 0)

    twin = (NEAR[2],) * 4

    def sum_src(far_parts, near_parts):
        near1, near3, sent, kept = near_parts
        got = [move(part, FAR, slot, True) for slot, part in enumerate(far_parts)]
        got += [move(near1, NEAR, 1, True), move(near3, NEAR, 3, True), move(sent, twin, 0, True)]
        total = kept.astype(f32)
        for part in got:
            total = total + part.astype(f32)
        return total

    def gather_src(shard):
        far = [move(shard, FAR, slot, False) for slot in (3, 2, 1, 0)][::-1]
        near3, near1 = (move(shard, NEAR, slot, False) for slot in (3, 1))
        mate = move(shard, twin, 0, False)
        near = [jnp.where(first, shard, mate), near1, jnp.where(first, mate, shard), near3]
        return near, far

    far_rows = [owner_row(FAR, slot) // block for slot in range(4)]
    near_rows = [owner_row(NEAR, slot) // block for slot in range(4)]
    own_row = (y * N_XL + x) * block
    twin_row = owner_row(twin, 0)
    far_parts = blocks_dot(
        encoder, 0, [bf16] * 4, source=residual_rows, order=jnp.stack(far_rows)
    )
    near_parts = blocks_dot(
        encoder,
        0,
        [bf16, bf16, bf16, f32],
        source=residual_rows,
        order=jnp.stack([near_rows[1], near_rows[3], twin_row // block, own_row // block]),
    )
    pre_act = sum_src(far_parts, near_parts) + enc_bias[None, :]
    latent = (jax.nn.softplus(SHARPNESS * pre_act) / SHARPNESS).astype(bf16)
    slope = jax.nn.sigmoid(SHARPNESS * pre_act)

    near, far = gather_src(latent)

    def core_sum(blocks):
        sent = dot(jnp.concatenate(blocks[2:], axis=0), decoder).astype(bf16)
        theirs = swap(sent, "core", N_CORE, 1)
        mine = dot(jnp.concatenate(blocks[:2], axis=0), decoder) + theirs.astype(f32)
        return mine.astype(bf16), sent

    rows = 4 * block // N_RING
    near_sum, theirs_done = core_sum(near)
    far_blocks = lax.optimization_barrier(tuple(far) + (theirs_done, near[1]))[:4]
    far_sum, _ = core_sum(far_blocks)
    shares = jnp.concatenate([near_sum, far_sum], axis=0)
    weights, shares = lax.optimization_barrier((decoder, shares))
    squares = jnp.sum(jnp.square(weights.astype(f32)), axis=1)
    shares = lax.all_to_all(shares.reshape(N_RING, rows, -1), RING, 0, 0)

    own_sq = squares + swap(squares, "xl", N_XL, 1)
    own_sq = own_sq + swap(own_sq, "y", N_Y, 1)
    other_sq = swap(own_sq, "y", N_Y, 2)
    own_norm = jnp.sqrt(own_sq + EPSILON)
    penalty = PENALTY * (own_norm + jnp.sqrt(other_sq + EPSILON))
    dec_bias, own_norm, penalty = lax.optimization_barrier((dec_bias, own_norm, penalty))

    recon = jnp.broadcast_to(dec_bias[None, :], shares.shape[1:])
    for i in range(N_RING):
        recon = recon + shares[i].astype(f32)
    per_block = N_RING // 4
    starts = jnp.stack([owner_row(o, slot) for o in (NEAR, FAR) for slot in range(2)])
    start = lax.dynamic_index_in_dim(starts, ring // per_block, 0, False)
    target = rows_of(start + (ring % per_block) * rows, rows)
    errors = (recon - target.astype(f32)).astype(bf16)
    order = jnp.stack(near_rows + far_rows)
    order, errors = lax.optimization_barrier((order, errors))
    res_t = transpose(residual_rows, order, block)
    errors = jnp.broadcast_to(errors[None], (N_RING,) + errors.shape)
    mine = lax.all_to_all(errors, RING, 0, 0).reshape(4, block, -1)
    mine, res_t = lax.optimization_barrier((mine, res_t))
    theirs = swap(mine, "core", N_CORE, 1)
    near_err = [mine[0], mine[1], theirs[0], theirs[1]]
    far_err = [mine[2], mine[3], theirs[2], theirs[3]]

    types = [bf16] * 4
    far0, far1, near1, low = blocks_dot(
        decoder, 1, types, blocks=[far_err[0], far_err[1], near_err[1], near_err[0]]
    )
    far2, far3, near3, high = blocks_dot(
        decoder, 1, types, blocks=[far_err[2], far_err[3], near_err[3], near_err[2]]
    )
    sent, kept = jnp.where(first, high, low), jnp.where(first, low, high)
    act_grad = sum_src([far0, far1, far2, far3], [near1, near3, sent, kept]) + penalty[None, :]
    grad_decoder = decoder_grad(
        near + far, near_err + far_err, decoder, jnp.stack([own_norm] * 8), loss_scale
    )
    slope, grad_decoder = lax.optimization_barrier((slope, grad_decoder))
    grad_pre = (loss_scale * act_grad * slope).astype(bf16)
    near_grad, far_grad = gather_src(grad_pre)

    grad_encoder = encoder_grad(res_t, near_grad, 0, None)
    grad_encoder = encoder_grad(res_t, far_grad, 1, grad_encoder)
    return (grad_encoder, grad_decoder)


def solution(mesh):
    fine = Mesh(mesh.devices.reshape(SHAPE), NAMES)
    in_specs = (P(None, SRC), P(SRC, LAT), P(LAT, SRC), P(LAT), P(SRC))
    out_specs = (P(SRC, LAT), P(LAT, SRC))
    return jax.shard_map(
        per_device, mesh=fine, in_specs=in_specs, out_specs=out_specs, check_vma=False
    )
```

```python
import math

import jax
import jax.numpy as jnp
from jax import lax
from jax.experimental import pallas as pl
from jax.experimental.pallas import tpu as pltpu
from jax.sharding import Mesh
from jax.sharding import PartitionSpec as P

D = 4096
SRCS = 2

SHARPNESS = 8.0
PENALTY = 1.0
EPSILON = 1e-06

NAMES = ("y", "xl", "xh", "z", "core")
SHAPE = (4, 2, 2, 8, 2)
N_Y, N_XL, N_XH, N_Z, N_CORE = SHAPE
SRC = ("y", "xl")
LAT = ("xh", "z", "core")
RING = ("xh", "z")
N_SRC = N_Y * N_XL
N_RING = N_XH * N_Z

NEAR = ((0, 0), (0, 1), (1, 0), (3, 0))
FAR = ((2, 0), (1, 1), (3, 1), (2, 1))

bf16 = jnp.bfloat16
f32 = jnp.float32


def swap(value, axis, size, mask):
    return lax.ppermute(value, axis, [(i, i ^ mask) for i in range(size)])


def place(offsets, slot, core):
    return offsets[(slot + 2 * core) % 4]


def behind(y, x, offset):
    return (y - offset[0]) % N_Y, x ^ offset[1]


def move(value, offsets, slot, to_owner):
    pairs = []
    for y in range(N_Y):
        for x in range(N_XL):
            for core in range(N_CORE):
                oy, ox = behind(y, x, place(offsets, slot, core))
                here = (y * N_XL + x) * N_CORE + core
                there = (oy * N_XL + ox) * N_CORE + core
                pairs.append((here, there) if to_owner else (there, here))
    return lax.ppermute(value, ("y", "xl", "core"), pairs)


def dot(a, b):
    return jnp.dot(a, b, preferred_element_type=f32)


def dot_t(a, b):
    return jnp.einsum("bk,jk->bj", a, b, preferred_element_type=f32)


def blocks_dot(weight, contract, dtypes, blocks=None, source=None, order=None):
    n = len(dtypes)
    tile = 256
    depth = weight.shape[contract]
    width = weight.shape[1 - contract]
    block = blocks[0].shape[0] if source is None else source.shape[0] // N_SRC

    def kernel(order_ref, *refs):
        ins, w_ref, outs, all_ref = refs[:n], refs[n], refs[n + 1 : 2 * n + 1], refs[-1]

        @pl.when(pl.program_id(0) == 0)
        def _():
            for i in range(n):
                all_ref[i * block : (i + 1) * block] = ins[i][...]

        product = lax.dot_general(
            all_ref[...], w_ref[...], (((1,), (contract,)), ((), ())), preferred_element_type=f32
        )
        for i in range(n):
            outs[i][...] = product[i * block : (i + 1) * block].astype(outs[i].dtype)

    if source is None:
        order = jnp.zeros((1,), jnp.int32)
        in_specs = [pl.BlockSpec((block, depth), lambda i, o: (0, 0))] * n
    else:
        blocks = [source] * n
        in_specs = [pl.BlockSpec((block, depth), lambda i, o, p=p: (o[p], 0)) for p in range(n)]
    if contract == 0:
        w_spec = pl.BlockSpec((depth, tile), lambda i, o: (0, i))
    else:
        w_spec = pl.BlockSpec((tile, depth), lambda i, o: (i, 0))
    return pl.pallas_call(
        kernel,
        grid_spec=pltpu.PrefetchScalarGridSpec(
            num_scalar_prefetch=1,
            grid=(width // tile,),
            in_specs=in_specs + [w_spec],
            out_specs=[pl.BlockSpec((block, tile), lambda i, o: (0, i))] * n,
            scratch_shapes=[pltpu.VMEM((n * block, depth), bf16)],
        ),
        out_shape=[jax.ShapeDtypeStruct((block, width), d) for d in dtypes],
        name="blocks_dot",
    )(order, *blocks, weight)


def decoder_grad(latents, errors, decoder, norms, loss_scale):
    n = len(latents)
    width, feat = decoder.shape
    block = latents[0].shape[0]
    rows = n * block
    tile = 256

    def kernel(*refs):
        lat, err = refs[:n], refs[n : 2 * n]
        dec_ref, norm_ref, out_ref, err_all = refs[2 * n :]

        @pl.when(pl.program_id(0) == 0)
        def _():
            for i in range(n):
                err_all[i * block : (i + 1) * block] = err[i][...]

        tall = jnp.concatenate([l_ref[...] for l_ref in lat], axis=0).T
        outer = jnp.dot(tall, err_all[...], preferred_element_type=f32)
        ones = jnp.ones((rows, 128), bf16)
        sums = jnp.dot(tall, ones, preferred_element_type=f32)[:, :1]
        shrink = loss_scale * PENALTY * sums / norm_ref[...].T[:, :1]
        out_ref[...] = (loss_scale * outer + shrink * dec_ref[...].astype(f32)).astype(bf16)

    return pl.pallas_call(
        kernel,
        grid=(width // tile,),
        in_specs=[pl.BlockSpec((block, tile), lambda i: (0, i))] * n
        + [pl.BlockSpec((block, feat), lambda i: (0, 0))] * n
        + [
            pl.BlockSpec((tile, feat), lambda i: (i, 0)),
            pl.BlockSpec((8, tile), lambda i: (0, i)),
        ],
        out_specs=pl.BlockSpec((tile, feat), lambda i: (i, 0)),
        out_shape=jax.ShapeDtypeStruct(decoder.shape, bf16),
        scratch_shapes=[pltpu.VMEM((rows, feat), bf16)],
        name="decoder_grad",
    )(*latents, *errors, decoder, norms)


def transpose(value, order, block):
    rows, cols = value.shape

    def kernel(order_ref, in_ref, out_ref):
        out_ref[...] = in_ref[...].T

    return pl.pallas_call(
        kernel,
        grid_spec=pltpu.PrefetchScalarGridSpec(
            num_scalar_prefetch=1,
            grid=(rows // block,),
            in_specs=[pl.BlockSpec((block, cols), lambda i, order_ref: (order_ref[i], 0))],
            out_specs=pl.BlockSpec((cols, block), lambda i, order_ref: (0, i)),
        ),
        out_shape=jax.ShapeDtypeStruct((cols, rows), value.dtype),
        name="transpose",
    )(order, value)


def encoder_grad(res_t, grads, part, so_far):
    n = len(grads)
    feat = res_t.shape[0]
    block, width = grads[0].shape
    tile = 256
    last = so_far is not None

    def kernel(res_ref, *refs):
        out_ref, grad_all = refs[-2:]

        @pl.when(pl.program_id(0) == 0)
        def _():
            for i in range(n):
                grad_all[i * block : (i + 1) * block] = refs[i][...]

        total = jnp.dot(res_ref[...], grad_all[...], preferred_element_type=f32)
        if last:
            total += refs[n][...]
        out_ref[...] = total.astype(out_ref.dtype)

    spec = pl.BlockSpec((tile, width), lambda i: (i, 0))
    return pl.pallas_call(
        kernel,
        grid=(feat // tile,),
        in_specs=[pl.BlockSpec((tile, n * block), lambda i: (i, part))]
        + [pl.BlockSpec((block, width), lambda i: (0, 0))] * n
        + [spec] * last,
        out_specs=spec,
        out_shape=jax.ShapeDtypeStruct((feat, width), bf16 if last else f32),
        scratch_shapes=[pltpu.VMEM((n * block, width), bf16)],
        name="encoder_grad",
    )(res_t, *grads, *([so_far] if last else []))


def per_device(residual_rows, encoder, decoder, enc_bias, dec_bias):
    row_count = residual_rows.shape[0]
    loss_scale = 1.0 / math.sqrt(row_count)
    block = row_count // N_SRC
    y, x, core = (lax.axis_index(a) for a in ("y", "xl", "core"))
    ring = lax.axis_index(RING)
    first = core == 0

    def owner_row(offsets, slot):
        rows = []
        for c in range(N_CORE):
            oy, ox = behind(y, x, place(offsets, slot, c))
            rows.append((oy * N_XL + ox) * block)
        return jnp.where(first, rows[0], rows[1])

    def rows_of(start, count):
        return lax.dynamic_slice_in_dim(residual_rows, start, count, 0)

    twin = (NEAR[2],) * 4
    own_row = (y * N_XL + x) * block

    def sum_src(far_parts, near_parts):
        near1, near3, sent, kept = near_parts
        got = [move(part, FAR, slot, True) for slot, part in enumerate(far_parts)]
        got += [move(near1, NEAR, 1, True), move(near3, NEAR, 3, True), move(sent, twin, 0, True)]
        total = kept.astype(f32)
        for part in got:
            total = total + part.astype(f32)
        return total

    def gather_src(shard, work=None, seed=None):
        near3, near1 = (move(shard, NEAR, slot, False) for slot in (3, 1))
        mate = move(shard, twin, 0, False)
        late, done = shard, None
        if work is not None:
            near1, seed = lax.optimization_barrier((near1, seed))
            done = work(seed)
            late, done = lax.optimization_barrier((shard, done))
        far = [
            move(late if slot > 1 else shard, FAR, slot, False) for slot in (3, 2, 1, 0)
        ][::-1]
        near = [jnp.where(first, shard, mate), near1, jnp.where(first, mate, shard), near3]
        return near, far, done

    far_rows = [owner_row(FAR, slot) // block for slot in range(4)]
    near_rows = [owner_row(NEAR, slot) // block for slot in range(4)]
    twin_row = owner_row(twin, 0)
    far_parts = blocks_dot(
        encoder, 0, [bf16] * 4, source=residual_rows, order=jnp.stack(far_rows)
    )
    near_parts = blocks_dot(
        encoder,
        0,
        [bf16, bf16, bf16, f32],
        source=residual_rows,
        order=jnp.stack([near_rows[1], near_rows[3], twin_row // block, own_row // block]),
    )
    pre_act = sum_src(far_parts, near_parts) + enc_bias[None, :]
    latent = (jax.nn.softplus(SHARPNESS * pre_act) / SHARPNESS).astype(bf16)
    slope = jax.nn.sigmoid(SHARPNESS * pre_act)

    near, far, _ = gather_src(latent)

    def core_sum(blocks):
        sent = dot(jnp.concatenate(blocks[2:], axis=0), decoder).astype(bf16)
        theirs = swap(sent, "core", N_CORE, 1)
        mine = dot(jnp.concatenate(blocks[:2], axis=0), decoder) + theirs.astype(f32)
        return mine.astype(bf16), sent

    rows = 4 * block // N_RING
    near_sum, theirs_done = core_sum(near)
    far_blocks = lax.optimization_barrier(tuple(far) + (theirs_done, near[1]))[:4]
    far_sum, _ = core_sum(far_blocks)
    shares = jnp.concatenate([near_sum, far_sum], axis=0)
    weights, shares = lax.optimization_barrier((decoder, shares))
    squares = jnp.sum(jnp.square(weights.astype(f32)), axis=1)
    shares = lax.all_to_all(shares.reshape(N_RING, rows, -1), RING, 0, 0)

    own_sq = squares + swap(squares, "xl", N_XL, 1)
    own_sq = own_sq + swap(own_sq, "y", N_Y, 1)
    other_sq = swap(own_sq, "y", N_Y, 2)
    own_norm = jnp.sqrt(own_sq + EPSILON)
    penalty = PENALTY * (own_norm + jnp.sqrt(other_sq + EPSILON))
    dec_bias, own_norm, penalty = lax.optimization_barrier((dec_bias, own_norm, penalty))

    recon = jnp.broadcast_to(dec_bias[None, :], shares.shape[1:])
    for i in range(N_RING):
        recon = recon + shares[i].astype(f32)
    per_block = N_RING // 4
    starts = jnp.stack([owner_row(o, slot) for o in (NEAR, FAR) for slot in range(2)])
    start = lax.dynamic_index_in_dim(starts, ring // per_block, 0, False)
    target = rows_of(start + (ring % per_block) * rows, rows)
    errors = (recon - target.astype(f32)).astype(bf16)
    order = jnp.stack(near_rows + far_rows)
    order, errors = lax.optimization_barrier((order, errors))
    res_t = transpose(residual_rows, order, block)
    errors = jnp.broadcast_to(errors[None], (N_RING,) + errors.shape)
    mine = lax.all_to_all(errors, RING, 0, 0).reshape(4, block, -1)
    mine, res_t = lax.optimization_barrier((mine, res_t))
    theirs = swap(mine, "core", N_CORE, 1)
    near_err = [mine[0], mine[1], theirs[0], theirs[1]]
    far_err = [mine[2], mine[3], theirs[2], theirs[3]]

    far0, far1, near1 = (
        dot_t(e, decoder).astype(bf16) for e in (far_err[0], far_err[1], near_err[1])
    )
    far2, far3, near3, high, low = blocks_dot(
        decoder,
        1,
        [bf16] * 5,
        blocks=[far_err[2], far_err[3], near_err[3], near_err[2], near_err[0]],
    )
    sent, kept = jnp.where(first, high, low), jnp.where(first, low, high)
    act_grad = sum_src([far0, far1, far2, far3], [near1, near3, sent, kept]) + penalty[None, :]
    grad_pre = (loss_scale * act_grad * slope).astype(bf16)
    def work(norms):
        return decoder_grad(
            near + far, near_err + far_err, decoder, jnp.stack([norms] * 8), loss_scale
        )

    near_grad, far_grad, grad_decoder = gather_src(grad_pre, work, own_norm)

    grad_encoder = encoder_grad(res_t, near_grad, 0, None)
    grad_encoder = encoder_grad(res_t, far_grad, 1, grad_encoder)
    return (grad_encoder, grad_decoder)


def solution(mesh):
    fine = Mesh(mesh.devices.reshape(SHAPE), NAMES)
    in_specs = (P(None, SRC), P(SRC, LAT), P(LAT, SRC), P(LAT), P(SRC))
    out_specs = (P(SRC, LAT), P(LAT, SRC))
    return jax.shard_map(
        per_device, mesh=fine, in_specs=in_specs, out_specs=out_specs, check_vma=False
    )
```

```python
import math

import jax
import jax.numpy as jnp
from jax import lax
from jax.experimental import pallas as pl
from jax.experimental.pallas import tpu as pltpu
from jax.sharding import Mesh
from jax.sharding import PartitionSpec as P

D = 4096
SRCS = 2

SHARPNESS = 8.0
PENALTY = 1.0
EPSILON = 1e-06

NAMES = ("y", "xl", "xh", "z", "core")
SHAPE = (4, 2, 2, 8, 2)
N_Y, N_XL, N_XH, N_Z, N_CORE = SHAPE
SRC = ("y", "xl")
LAT = ("xh", "z", "core")
RING = ("xh", "z")
N_SRC = N_Y * N_XL
N_RING = N_XH * N_Z

NEAR = ((0, 0), (0, 1), (1, 0), (3, 0))
FAR = ((2, 0), (1, 1), (3, 1), (2, 1))

bf16 = jnp.bfloat16
f32 = jnp.float32


def swap(value, axis, size, mask):
    return lax.ppermute(value, axis, [(i, i ^ mask) for i in range(size)])


def place(offsets, slot, core):
    return offsets[(slot + 2 * core) % 4]


def behind(y, x, offset):
    return (y - offset[0]) % N_Y, x ^ offset[1]


def move(value, offsets, slot, to_owner):
    pairs = []
    for y in range(N_Y):
        for x in range(N_XL):
            for core in range(N_CORE):
                oy, ox = behind(y, x, place(offsets, slot, core))
                here = (y * N_XL + x) * N_CORE + core
                there = (oy * N_XL + ox) * N_CORE + core
                pairs.append((here, there) if to_owner else (there, here))
    return lax.ppermute(value, ("y", "xl", "core"), pairs)


def dot(a, b):
    return jnp.dot(a, b, preferred_element_type=f32)


def dot_t(a, b):
    return jnp.einsum("bk,jk->bj", a, b, preferred_element_type=f32)


def blocks_dot(weight, contract, dtypes, blocks=None, source=None, order=None):
    n = len(dtypes)
    tile = 256
    depth = weight.shape[contract]
    width = weight.shape[1 - contract]
    block = blocks[0].shape[0] if source is None else source.shape[0] // N_SRC

    def kernel(order_ref, *refs):
        ins, w_ref, outs, all_ref = refs[:n], refs[n], refs[n + 1 : 2 * n + 1], refs[-1]

        @pl.when(pl.program_id(0) == 0)
        def _():
            for i in range(n):
                all_ref[i * block : (i + 1) * block] = ins[i][...]

        product = lax.dot_general(
            all_ref[...], w_ref[...], (((1,), (contract,)), ((), ())), preferred_element_type=f32
        )
        for i in range(n):
            outs[i][...] = product[i * block : (i + 1) * block].astype(outs[i].dtype)

    if source is None:
        order = jnp.zeros((1,), jnp.int32)
        in_specs = [pl.BlockSpec((block, depth), lambda i, o: (0, 0))] * n
    else:
        blocks = [source] * n
        in_specs = [pl.BlockSpec((block, depth), lambda i, o, p=p: (o[p], 0)) for p in range(n)]
    if contract == 0:
        w_spec = pl.BlockSpec((depth, tile), lambda i, o: (0, i))
    else:
        w_spec = pl.BlockSpec((tile, depth), lambda i, o: (i, 0))
    return pl.pallas_call(
        kernel,
        grid_spec=pltpu.PrefetchScalarGridSpec(
            num_scalar_prefetch=1,
            grid=(width // tile,),
            in_specs=in_specs + [w_spec],
            out_specs=[pl.BlockSpec((block, tile), lambda i, o: (0, i))] * n,
            scratch_shapes=[pltpu.VMEM((n * block, depth), bf16)],
        ),
        out_shape=[jax.ShapeDtypeStruct((block, width), d) for d in dtypes],
        name="blocks_dot",
    )(order, *blocks, weight)


def decoder_grad(latents, errors, decoder, norms, loss_scale):
    n = len(latents)
    width, feat = decoder.shape
    block = latents[0].shape[0]
    rows = n * block
    tile, span = 256, 512

    def kernel(*refs):
        lat, err = refs[:n], refs[n : 2 * n]
        dec_ref, norm_ref, out_ref, err_all, tall_ref, shrink_ref = refs[2 * n :]

        @pl.when((pl.program_id(0) == 0) & (pl.program_id(1) == 0))
        def _():
            for i in range(n):
                err_all[i * block : (i + 1) * block] = err[i][...]

        @pl.when(pl.program_id(1) == 0)
        def _():
            tall_ref[...] = jnp.concatenate([l_ref[...] for l_ref in lat], axis=0).T
            ones = jnp.ones((rows, 128), bf16)
            sums = jnp.dot(tall_ref[...], ones, preferred_element_type=f32)
            shrink_ref[...] = loss_scale * PENALTY * sums / norm_ref[...].T[:, :1]

        cols = pl.ds(pl.multiple_of(pl.program_id(1) * span, span), span)
        outer = jnp.dot(tall_ref[...], err_all[:, cols], preferred_element_type=f32)
        out_ref[...] = (
            loss_scale * outer + shrink_ref[:, :1] * dec_ref[...].astype(f32)
        ).astype(bf16)

    return pl.pallas_call(
        kernel,
        grid=(width // tile, feat // span),
        in_specs=[pl.BlockSpec((block, tile), lambda i, k: (0, i))] * n
        + [pl.BlockSpec((block, feat), lambda i, k: (0, 0))] * n
        + [
            pl.BlockSpec((tile, span), lambda i, k: (i, k)),
            pl.BlockSpec((8, tile), lambda i, k: (0, i)),
        ],
        out_specs=pl.BlockSpec((tile, span), lambda i, k: (i, k)),
        out_shape=jax.ShapeDtypeStruct(decoder.shape, bf16),
        scratch_shapes=[
            pltpu.VMEM((rows, feat), bf16),
            pltpu.VMEM((tile, rows), bf16),
            pltpu.VMEM((tile, 128), f32),
        ],
        name="decoder_grad",
    )(*latents, *errors, decoder, norms)


def transpose(value, order, block):
    rows, cols = value.shape

    def kernel(order_ref, in_ref, out_ref):
        out_ref[...] = in_ref[...].T

    return pl.pallas_call(
        kernel,
        grid_spec=pltpu.PrefetchScalarGridSpec(
            num_scalar_prefetch=1,
            grid=(rows // block,),
            in_specs=[pl.BlockSpec((block, cols), lambda i, order_ref: (order_ref[i], 0))],
            out_specs=pl.BlockSpec((cols, block), lambda i, order_ref: (0, i)),
        ),
        out_shape=jax.ShapeDtypeStruct((cols, rows), value.dtype),
        name="transpose",
    )(order, value)


def encoder_grad(res_t, grads, part, so_far):
    n = len(grads)
    feat = res_t.shape[0]
    block, width = grads[0].shape
    tile = 256
    last = so_far is not None

    def kernel(res_ref, *refs):
        out_ref, grad_all = refs[-2:]

        @pl.when(pl.program_id(0) == 0)
        def _():
            for i in range(n):
                grad_all[i * block : (i + 1) * block] = refs[i][...]

        total = jnp.dot(res_ref[...], grad_all[...], preferred_element_type=f32)
        if last:
            total += refs[n][...]
        out_ref[...] = total.astype(out_ref.dtype)

    spec = pl.BlockSpec((tile, width), lambda i: (i, 0))
    return pl.pallas_call(
        kernel,
        grid=(feat // tile,),
        in_specs=[pl.BlockSpec((tile, n * block), lambda i: (i, part))]
        + [pl.BlockSpec((block, width), lambda i: (0, 0))] * n
        + [spec] * last,
        out_specs=spec,
        out_shape=jax.ShapeDtypeStruct((feat, width), bf16 if last else f32),
        scratch_shapes=[pltpu.VMEM((n * block, width), bf16)],
        name="encoder_grad",
    )(res_t, *grads, *([so_far] if last else []))


def per_device(residual_rows, encoder, decoder, enc_bias, dec_bias):
    row_count = residual_rows.shape[0]
    loss_scale = 1.0 / math.sqrt(row_count)
    block = row_count // N_SRC
    y, x, core = (lax.axis_index(a) for a in ("y", "xl", "core"))
    ring = lax.axis_index(RING)
    first = core == 0

    def owner_row(offsets, slot):
        rows = []
        for c in range(N_CORE):
            oy, ox = behind(y, x, place(offsets, slot, c))
            rows.append((oy * N_XL + ox) * block)
        return jnp.where(first, rows[0], rows[1])

    def rows_of(start, count):
        return lax.dynamic_slice_in_dim(residual_rows, start, count, 0)

    twin = (NEAR[2],) * 4

    def sum_src(far_parts, near_parts):
        near1, near3, sent, kept = near_parts
        got = [move(part, FAR, slot, True) for slot, part in enumerate(far_parts)]
        got += [move(near1, NEAR, 1, True), move(near3, NEAR, 3, True), move(sent, twin, 0, True)]
        total = kept.astype(f32)
        for part in got:
            total = total + part.astype(f32)
        return total

    def gather_src(shard):
        far = [move(shard, FAR, slot, False) for slot in (3, 2, 1, 0)][::-1]
        near3, near1 = (move(shard, NEAR, slot, False) for slot in (3, 1))
        mate = move(shard, twin, 0, False)
        near = [jnp.where(first, shard, mate), near1, jnp.where(first, mate, shard), near3]
        return near, far

    far_rows = [owner_row(FAR, slot) // block for slot in range(4)]
    near_rows = [owner_row(NEAR, slot) // block for slot in range(4)]
    own_row = (y * N_XL + x) * block
    twin_row = owner_row(twin, 0)
    far_parts = blocks_dot(
        encoder, 0, [bf16] * 4, source=residual_rows, order=jnp.stack(far_rows)
    )
    near_parts = blocks_dot(
        encoder,
        0,
        [bf16, bf16, bf16, f32],
        source=residual_rows,
        order=jnp.stack([near_rows[1], near_rows[3], twin_row // block, own_row // block]),
    )
    pre_act = sum_src(far_parts, near_parts) + enc_bias[None, :]
    latent = (jax.nn.softplus(SHARPNESS * pre_act) / SHARPNESS).astype(bf16)
    slope = jax.nn.sigmoid(SHARPNESS * pre_act)

    near, far = gather_src(latent)

    def core_sum(blocks):
        sent = dot(jnp.concatenate(blocks[2:], axis=0), decoder).astype(bf16)
        theirs = swap(sent, "core", N_CORE, 1)
        mine = dot(jnp.concatenate(blocks[:2], axis=0), decoder) + theirs.astype(f32)
        return mine.astype(bf16), sent

    rows = 4 * block // N_RING
    near_sum, theirs_done = core_sum(near)
    far_blocks = lax.optimization_barrier(tuple(far) + (theirs_done, near[1]))[:4]
    far_sum, _ = core_sum(far_blocks)
    shares = jnp.concatenate([near_sum, far_sum], axis=0)
    weights, shares = lax.optimization_barrier((decoder, shares))
    squares = jnp.sum(jnp.square(weights.astype(f32)), axis=1)
    shares = lax.all_to_all(shares.reshape(N_RING, rows, -1), RING, 0, 0)

    own_sq = squares + swap(squares, "xl", N_XL, 1)
    own_sq = own_sq + swap(own_sq, "y", N_Y, 1)
    other_sq = swap(own_sq, "y", N_Y, 2)
    own_norm = jnp.sqrt(own_sq + EPSILON)
    penalty = PENALTY * (own_norm + jnp.sqrt(other_sq + EPSILON))
    dec_bias, own_norm, penalty = lax.optimization_barrier((dec_bias, own_norm, penalty))

    recon = jnp.broadcast_to(dec_bias[None, :], shares.shape[1:])
    for i in range(N_RING):
        recon = recon + shares[i].astype(f32)
    per_block = N_RING // 4
    starts = jnp.stack([owner_row(o, slot) for o in (NEAR, FAR) for slot in range(2)])
    start = lax.dynamic_index_in_dim(starts, ring // per_block, 0, False)
    target = rows_of(start + (ring % per_block) * rows, rows)
    errors = (recon - target.astype(f32)).astype(bf16)
    order = jnp.stack(near_rows + far_rows)
    order, errors = lax.optimization_barrier((order, errors))
    res_t = transpose(residual_rows, order, block)
    errors = jnp.broadcast_to(errors[None], (N_RING,) + errors.shape)
    mine = lax.all_to_all(errors, RING, 0, 0).reshape(4, block, -1)
    mine, res_t = lax.optimization_barrier((mine, res_t))
    theirs = swap(mine, "core", N_CORE, 1)
    near_err = [mine[0], mine[1], theirs[0], theirs[1]]
    far_err = [mine[2], mine[3], theirs[2], theirs[3]]

    sent = jnp.where(first, near_err[2], near_err[0])
    kept = jnp.where(first, near_err[0], near_err[2])
    far_back = [dot_t(e, decoder).astype(bf16) for e in far_err]
    near1 = dot_t(near_err[1], decoder).astype(bf16)
    sent, far_back[2], far_back[3] = lax.optimization_barrier((sent, far_back[2], far_back[3]))
    near3, sent, kept = blocks_dot(
        decoder, 1, [bf16, bf16, f32], blocks=[near_err[3], sent, kept]
    )
    near_back = [near1, near3, sent, kept]
    act_grad = sum_src(far_back, near_back) + penalty[None, :]
    grad_decoder = decoder_grad(
        near + far, near_err + far_err, decoder, jnp.stack([own_norm] * 8), loss_scale
    )
    slope, grad_decoder = lax.optimization_barrier((slope, grad_decoder))
    grad_pre = (loss_scale * act_grad * slope).astype(bf16)
    near_grad, far_grad = gather_src(grad_pre)

    grad_encoder = encoder_grad(res_t, near_grad, 0, None)
    grad_encoder = encoder_grad(res_t, far_grad, 1, grad_encoder)
    return (grad_encoder, grad_decoder)


def solution(mesh):
    fine = Mesh(mesh.devices.reshape(SHAPE), NAMES)
    in_specs = (P(None, SRC), P(SRC, LAT), P(LAT, SRC), P(LAT), P(SRC))
    out_specs = (P(SRC, LAT), P(LAT, SRC))
    return jax.shard_map(
        per_device, mesh=fine, in_specs=in_specs, out_specs=out_specs, check_vma=False
    )
```

```python
import math

import jax
import jax.numpy as jnp
from jax import lax
from jax.experimental import pallas as pl
from jax.experimental.pallas import tpu as pltpu
from jax.sharding import Mesh
from jax.sharding import PartitionSpec as P

D = 4096
SRCS = 2

SHARPNESS = 8.0
PENALTY = 1.0
EPSILON = 1e-06

NAMES = ("y", "xl", "xh", "z", "core")
SHAPE = (4, 2, 2, 8, 2)
N_Y, N_XL, N_XH, N_Z, N_CORE = SHAPE
SRC = ("y", "xl")
LAT = ("xh", "z", "core")
RING = ("xh", "z")
N_SRC = N_Y * N_XL
N_RING = N_XH * N_Z

NEAR = ((0, 0), (0, 1), (1, 0), (3, 0))
FAR = ((2, 0), (1, 1), (3, 1), (2, 1))

bf16 = jnp.bfloat16
f32 = jnp.float32


def swap(value, axis, size, mask):
    return lax.ppermute(value, axis, [(i, i ^ mask) for i in range(size)])


def place(offsets, slot, core):
    return offsets[(slot + 2 * core) % 4]


def behind(y, x, offset):
    return (y - offset[0]) % N_Y, x ^ offset[1]


def move(value, offsets, slot, to_owner):
    pairs = []
    for y in range(N_Y):
        for x in range(N_XL):
            for core in range(N_CORE):
                oy, ox = behind(y, x, place(offsets, slot, core))
                here = (y * N_XL + x) * N_CORE + core
                there = (oy * N_XL + ox) * N_CORE + core
                pairs.append((here, there) if to_owner else (there, here))
    return lax.ppermute(value, ("y", "xl", "core"), pairs)


def dot(a, b):
    return jnp.dot(a, b, preferred_element_type=f32)


def dot_t(a, b):
    return jnp.einsum("bk,jk->bj", a, b, preferred_element_type=f32)


def blocks_dot(weight, contract, dtypes, blocks=None, source=None, order=None):
    n = len(dtypes)
    tile = 256
    depth = weight.shape[contract]
    width = weight.shape[1 - contract]
    block = blocks[0].shape[0] if source is None else source.shape[0] // N_SRC

    def kernel(order_ref, *refs):
        ins, w_ref, outs, all_ref = refs[:n], refs[n], refs[n + 1 : 2 * n + 1], refs[-1]

        @pl.when(pl.program_id(0) == 0)
        def _():
            for i in range(n):
                all_ref[i * block : (i + 1) * block] = ins[i][...]

        product = lax.dot_general(
            all_ref[...], w_ref[...], (((1,), (contract,)), ((), ())), preferred_element_type=f32
        )
        for i in range(n):
            outs[i][...] = product[i * block : (i + 1) * block].astype(outs[i].dtype)

    if source is None:
        order = jnp.zeros((1,), jnp.int32)
        in_specs = [pl.BlockSpec((block, depth), lambda i, o: (0, 0))] * n
    else:
        blocks = [source] * n
        in_specs = [pl.BlockSpec((block, depth), lambda i, o, p=p: (o[p], 0)) for p in range(n)]
    if contract == 0:
        w_spec = pl.BlockSpec((depth, tile), lambda i, o: (0, i))
    else:
        w_spec = pl.BlockSpec((tile, depth), lambda i, o: (i, 0))
    return pl.pallas_call(
        kernel,
        grid_spec=pltpu.PrefetchScalarGridSpec(
            num_scalar_prefetch=1,
            grid=(width // tile,),
            in_specs=in_specs + [w_spec],
            out_specs=[pl.BlockSpec((block, tile), lambda i, o: (0, i))] * n,
            scratch_shapes=[pltpu.VMEM((n * block, depth), bf16)],
        ),
        out_shape=[jax.ShapeDtypeStruct((block, width), d) for d in dtypes],
        name="blocks_dot",
    )(order, *blocks, weight)


def decoder_grad(latents, errors, decoder, norms, loss_scale):
    n = len(latents)
    width, feat = decoder.shape
    block = latents[0].shape[0]
    rows = n * block
    tile = 256

    def kernel(*refs):
        lat, err = refs[:n], refs[n : 2 * n]
        dec_ref, norm_ref, out_ref, err_all = refs[2 * n :]

        @pl.when(pl.program_id(0) == 0)
        def _():
            for i in range(n):
                err_all[i * block : (i + 1) * block] = err[i][...]

        tall = jnp.concatenate([l_ref[...] for l_ref in lat], axis=0).T
        outer = jnp.dot(tall, err_all[...], preferred_element_type=f32)
        ones = jnp.ones((rows, 128), bf16)
        sums = jnp.dot(tall, ones, preferred_element_type=f32)[:, :1]
        shrink = loss_scale * PENALTY * sums / norm_ref[...].T[:, :1]
        out_ref[...] = (loss_scale * outer + shrink * dec_ref[...].astype(f32)).astype(bf16)

    return pl.pallas_call(
        kernel,
        grid=(width // tile,),
        in_specs=[pl.BlockSpec((block, tile), lambda i: (0, i))] * n
        + [pl.BlockSpec((block, feat), lambda i: (0, 0))] * n
        + [
            pl.BlockSpec((tile, feat), lambda i: (i, 0)),
            pl.BlockSpec((8, tile), lambda i: (0, i)),
        ],
        out_specs=pl.BlockSpec((tile, feat), lambda i: (i, 0)),
        out_shape=jax.ShapeDtypeStruct(decoder.shape, bf16),
        scratch_shapes=[pltpu.VMEM((rows, feat), bf16)],
        name="decoder_grad",
    )(*latents, *errors, decoder, norms)


def transpose(value, order, block):
    rows, cols = value.shape

    def kernel(order_ref, in_ref, out_ref):
        out_ref[...] = in_ref[...].T

    return pl.pallas_call(
        kernel,
        grid_spec=pltpu.PrefetchScalarGridSpec(
            num_scalar_prefetch=1,
            grid=(rows // block,),
            in_specs=[pl.BlockSpec((block, cols), lambda i, order_ref: (order_ref[i], 0))],
            out_specs=pl.BlockSpec((cols, block), lambda i, order_ref: (0, i)),
        ),
        out_shape=jax.ShapeDtypeStruct((cols, rows), value.dtype),
        name="transpose",
    )(order, value)


def encoder_grad(res_t, grads, part, so_far):
    n = len(grads)
    feat = res_t.shape[0]
    block, width = grads[0].shape
    tile = 256
    last = so_far is not None

    def kernel(res_ref, *refs):
        out_ref, grad_all = refs[-2:]

        @pl.when(pl.program_id(0) == 0)
        def _():
            for i in range(n):
                grad_all[i * block : (i + 1) * block] = refs[i][...]

        total = jnp.dot(res_ref[...], grad_all[...], preferred_element_type=f32)
        if last:
            total += refs[n][...]
        out_ref[...] = total.astype(out_ref.dtype)

    spec = pl.BlockSpec((tile, width), lambda i: (i, 0))
    return pl.pallas_call(
        kernel,
        grid=(feat // tile,),
        in_specs=[pl.BlockSpec((tile, n * block), lambda i: (i, part))]
        + [pl.BlockSpec((block, width), lambda i: (0, 0))] * n
        + [spec] * last,
        out_specs=spec,
        out_shape=jax.ShapeDtypeStruct((feat, width), bf16 if last else f32),
        scratch_shapes=[pltpu.VMEM((n * block, width), bf16)],
        name="encoder_grad",
    )(res_t, *grads, *([so_far] if last else []))


def per_device(residual_rows, encoder, decoder, enc_bias, dec_bias):
    row_count = residual_rows.shape[0]
    loss_scale = 1.0 / math.sqrt(row_count)
    block = row_count // N_SRC
    y, x, core = (lax.axis_index(a) for a in ("y", "xl", "core"))
    ring = lax.axis_index(RING)
    first = core == 0

    def owner_row(offsets, slot):
        rows = []
        for c in range(N_CORE):
            oy, ox = behind(y, x, place(offsets, slot, c))
            rows.append((oy * N_XL + ox) * block)
        return jnp.where(first, rows[0], rows[1])

    def rows_of(start, count):
        return lax.dynamic_slice_in_dim(residual_rows, start, count, 0)

    twin = (NEAR[2],) * 4

    def sum_src(far_parts, near_parts):
        near1, near3, sent, kept = near_parts
        got = [move(part, FAR, slot, True) for slot, part in enumerate(far_parts)]
        got += [move(near1, NEAR, 1, True), move(near3, NEAR, 3, True), move(sent, twin, 0, True)]
        total = kept.astype(f32)
        for part in got:
            total = total + part.astype(f32)
        return total

    def gather_src(shard):
        far = [move(shard, FAR, slot, False) for slot in (3, 2, 1, 0)][::-1]
        near3, near1 = (move(shard, NEAR, slot, False) for slot in (3, 1))
        mate = move(shard, twin, 0, False)
        near = [jnp.where(first, shard, mate), near1, jnp.where(first, mate, shard), near3]
        return near, far

    far_rows = [owner_row(FAR, slot) // block for slot in range(4)]
    near_rows = [owner_row(NEAR, slot) // block for slot in range(4)]
    own_row = (y * N_XL + x) * block
    twin_row = owner_row(twin, 0)
    far_parts = blocks_dot(
        encoder, 0, [bf16] * 4, source=residual_rows, order=jnp.stack(far_rows)
    )
    near_parts = blocks_dot(
        encoder,
        0,
        [bf16, bf16, bf16, f32],
        source=residual_rows,
        order=jnp.stack([near_rows[1], near_rows[3], twin_row // block, own_row // block]),
    )
    pre_act = sum_src(far_parts, near_parts) + enc_bias[None, :]
    latent = (jax.nn.softplus(SHARPNESS * pre_act) / SHARPNESS).astype(bf16)
    slope = jax.nn.sigmoid(SHARPNESS * pre_act)

    near, far = gather_src(latent)

    def core_sum(blocks):
        sent = dot(jnp.concatenate(blocks[2:], axis=0), decoder).astype(bf16)
        theirs = swap(sent, "core", N_CORE, 1)
        mine = dot(jnp.concatenate(blocks[:2], axis=0), decoder) + theirs.astype(f32)
        return mine.astype(bf16), sent

    rows = 4 * block // N_RING
    near_sum, theirs_done = core_sum(near)
    far_blocks = lax.optimization_barrier(tuple(far) + (theirs_done, near[1]))[:4]
    far_sum, _ = core_sum(far_blocks)
    shares = jnp.concatenate([near_sum, far_sum], axis=0)
    weights, shares = lax.optimization_barrier((decoder, shares))
    squares = jnp.sum(jnp.square(weights.astype(f32)), axis=1)
    shares = lax.all_to_all(shares.reshape(N_RING, rows, -1), RING, 0, 0)

    own_sq = squares + swap(squares, "xl", N_XL, 1)
    own_sq = own_sq + swap(own_sq, "y", N_Y, 1)
    other_sq = swap(own_sq, "y", N_Y, 2)
    own_norm = jnp.sqrt(own_sq + EPSILON)
    penalty = PENALTY * (own_norm + jnp.sqrt(other_sq + EPSILON))
    dec_bias, own_norm, penalty = lax.optimization_barrier((dec_bias, own_norm, penalty))

    recon = jnp.broadcast_to(dec_bias[None, :], shares.shape[1:])
    for i in range(N_RING):
        recon = recon + shares[i].astype(f32)
    per_block = N_RING // 4
    starts = jnp.stack([owner_row(o, slot) for o in (NEAR, FAR) for slot in range(2)])
    start = lax.dynamic_index_in_dim(starts, ring // per_block, 0, False)
    target = rows_of(start + (ring % per_block) * rows, rows)
    errors = (recon - target.astype(f32)).astype(bf16)
    order = jnp.stack(near_rows + far_rows)
    order, errors = lax.optimization_barrier((order, errors))
    res_t = transpose(residual_rows, order, block)
    errors = jnp.broadcast_to(errors[None], (N_RING,) + errors.shape)
    mine = lax.all_to_all(errors, RING, 0, 0).reshape(4, block, -1)
    mine, res_t = lax.optimization_barrier((mine, res_t))
    theirs = swap(mine, "core", N_CORE, 1)
    near_err = [mine[0], mine[1], theirs[0], theirs[1]]
    far_err = [mine[2], mine[3], theirs[2], theirs[3]]

    sent = jnp.where(first, near_err[2], near_err[0])
    kept = jnp.where(first, near_err[0], near_err[2])
    far_back = [dot_t(e, decoder).astype(bf16) for e in far_err]
    near_back = [
        dot_t(near_err[1], decoder).astype(bf16),
        dot_t(near_err[3], decoder).astype(bf16),
        dot_t(sent, decoder).astype(bf16),
        dot_t(kept, decoder),
    ]
    act_grad = sum_src(far_back, near_back) + penalty[None, :]
    grad_decoder = decoder_grad(
        near + far, near_err + far_err, decoder, jnp.stack([own_norm] * 8), loss_scale
    )
    slope, grad_decoder = lax.optimization_barrier((slope, grad_decoder))
    grad_pre = (loss_scale * act_grad * slope).astype(bf16)
    near_grad, far_grad = gather_src(grad_pre)

    grad_encoder = encoder_grad(res_t, near_grad, 0, None)
    grad_encoder = encoder_grad(res_t, far_grad, 1, grad_encoder)
    return (grad_encoder, grad_decoder)


def solution(mesh):
    fine = Mesh(mesh.devices.reshape(SHAPE), NAMES)
    in_specs = (P(None, SRC), P(SRC, LAT), P(LAT, SRC), P(LAT), P(SRC))
    out_specs = (P(SRC, LAT), P(LAT, SRC))
    return jax.shard_map(
        per_device, mesh=fine, in_specs=in_specs, out_specs=out_specs, check_vma=False
    )
```

```python
import math

import jax
import jax.numpy as jnp
from jax import lax
from jax.experimental import pallas as pl
from jax.experimental.pallas import tpu as pltpu
from jax.sharding import Mesh
from jax.sharding import PartitionSpec as P

D = 4096
SRCS = 2

SHARPNESS = 8.0
PENALTY = 1.0
EPSILON = 1e-06

NAMES = ("y", "xl", "xh", "z", "core")
SHAPE = (4, 2, 2, 8, 2)
N_Y, N_XL, N_XH, N_Z, N_CORE = SHAPE
SRC = ("y", "xl")
LAT = ("xh", "z", "core")
RING = ("xh", "z")
N_SRC = N_Y * N_XL
N_RING = N_XH * N_Z

NEAR = ((0, 0), (0, 1), (1, 0), (3, 0))
FAR = ((2, 0), (1, 1), (3, 1), (2, 1))

bf16 = jnp.bfloat16
f32 = jnp.float32


def swap(value, axis, size, mask):
    return lax.ppermute(value, axis, [(i, i ^ mask) for i in range(size)])


def place(offsets, slot, core):
    return offsets[(slot + 2 * core) % 4]


def behind(y, x, offset):
    return (y - offset[0]) % N_Y, x ^ offset[1]


def move(value, offsets, slot, to_owner):
    pairs = []
    for y in range(N_Y):
        for x in range(N_XL):
            for core in range(N_CORE):
                oy, ox = behind(y, x, place(offsets, slot, core))
                here = (y * N_XL + x) * N_CORE + core
                there = (oy * N_XL + ox) * N_CORE + core
                pairs.append((here, there) if to_owner else (there, here))
    return lax.ppermute(value, ("y", "xl", "core"), pairs)


def dot(a, b):
    return jnp.dot(a, b, preferred_element_type=f32)


def dot_t(a, b):
    return jnp.einsum("bk,jk->bj", a, b, preferred_element_type=f32)


def blocks_dot(weight, contract, dtypes, blocks=None, source=None, order=None):
    n = len(dtypes)
    tile = 256
    depth = weight.shape[contract]
    width = weight.shape[1 - contract]
    block = blocks[0].shape[0] if source is None else source.shape[0] // N_SRC

    def kernel(order_ref, *refs):
        ins, w_ref, outs, all_ref = refs[:n], refs[n], refs[n + 1 : 2 * n + 1], refs[-1]

        @pl.when(pl.program_id(0) == 0)
        def _():
            for i in range(n):
                all_ref[i * block : (i + 1) * block] = ins[i][...]

        product = lax.dot_general(
            all_ref[...], w_ref[...], (((1,), (contract,)), ((), ())), preferred_element_type=f32
        )
        for i in range(n):
            outs[i][...] = product[i * block : (i + 1) * block].astype(outs[i].dtype)

    if source is None:
        order = jnp.zeros((1,), jnp.int32)
        in_specs = [pl.BlockSpec((block, depth), lambda i, o: (0, 0))] * n
    else:
        blocks = [source] * n
        in_specs = [pl.BlockSpec((block, depth), lambda i, o, p=p: (o[p], 0)) for p in range(n)]
    if contract == 0:
        w_spec = pl.BlockSpec((depth, tile), lambda i, o: (0, i))
    else:
        w_spec = pl.BlockSpec((tile, depth), lambda i, o: (i, 0))
    return pl.pallas_call(
        kernel,
        grid_spec=pltpu.PrefetchScalarGridSpec(
            num_scalar_prefetch=1,
            grid=(width // tile,),
            in_specs=in_specs + [w_spec],
            out_specs=[pl.BlockSpec((block, tile), lambda i, o: (0, i))] * n,
            scratch_shapes=[pltpu.VMEM((n * block, depth), bf16)],
        ),
        out_shape=[jax.ShapeDtypeStruct((block, width), d) for d in dtypes],
        name="blocks_dot",
    )(order, *blocks, weight)


def decoder_grad(latents, errors, decoder, norms, loss_scale):
    n = len(latents)
    width, feat = decoder.shape
    block = latents[0].shape[0]
    rows = n * block
    tile = 256

    def kernel(*refs):
        lat, err = refs[:n], refs[n : 2 * n]
        dec_ref, norm_ref, out_ref, err_all = refs[2 * n :]

        @pl.when(pl.program_id(0) == 0)
        def _():
            for i in range(n):
                err_all[i * block : (i + 1) * block] = err[i][...]

        tall = jnp.concatenate([l_ref[...] for l_ref in lat], axis=0).T
        outer = jnp.dot(tall, err_all[...], preferred_element_type=f32)
        ones = jnp.ones((rows, 128), bf16)
        sums = jnp.dot(tall, ones, preferred_element_type=f32)[:, :1]
        shrink = loss_scale * PENALTY * sums / norm_ref[...].T[:, :1]
        out_ref[...] = (loss_scale * outer + shrink * dec_ref[...].astype(f32)).astype(bf16)

    return pl.pallas_call(
        kernel,
        grid=(width // tile,),
        in_specs=[pl.BlockSpec((block, tile), lambda i: (0, i))] * n
        + [pl.BlockSpec((block, feat), lambda i: (0, 0))] * n
        + [
            pl.BlockSpec((tile, feat), lambda i: (i, 0)),
            pl.BlockSpec((8, tile), lambda i: (0, i)),
        ],
        out_specs=pl.BlockSpec((tile, feat), lambda i: (i, 0)),
        out_shape=jax.ShapeDtypeStruct(decoder.shape, bf16),
        scratch_shapes=[pltpu.VMEM((rows, feat), bf16)],
        name="decoder_grad",
    )(*latents, *errors, decoder, norms)


def transpose(value, order, block):
    rows, cols = value.shape

    def kernel(order_ref, in_ref, out_ref):
        out_ref[...] = in_ref[...].T

    return pl.pallas_call(
        kernel,
        grid_spec=pltpu.PrefetchScalarGridSpec(
            num_scalar_prefetch=1,
            grid=(rows // block,),
            in_specs=[pl.BlockSpec((block, cols), lambda i, order_ref: (order_ref[i], 0))],
            out_specs=pl.BlockSpec((cols, block), lambda i, order_ref: (0, i)),
        ),
        out_shape=jax.ShapeDtypeStruct((cols, rows), value.dtype),
        name="transpose",
    )(order, value)


def encoder_grad(res_t, grads, part, so_far):
    n = len(grads)
    feat = res_t.shape[0]
    block, width = grads[0].shape
    tile = 256
    last = so_far is not None

    def kernel(res_ref, *refs):
        out_ref, grad_all = refs[-2:]

        @pl.when(pl.program_id(0) == 0)
        def _():
            for i in range(n):
                grad_all[i * block : (i + 1) * block] = refs[i][...]

        total = jnp.dot(res_ref[...], grad_all[...], preferred_element_type=f32)
        if last:
            total += refs[n][...]
        out_ref[...] = total.astype(out_ref.dtype)

    spec = pl.BlockSpec((tile, width), lambda i: (i, 0))
    return pl.pallas_call(
        kernel,
        grid=(feat // tile,),
        in_specs=[pl.BlockSpec((tile, n * block), lambda i: (i, part))]
        + [pl.BlockSpec((block, width), lambda i: (0, 0))] * n
        + [spec] * last,
        out_specs=spec,
        out_shape=jax.ShapeDtypeStruct((feat, width), bf16 if last else f32),
        scratch_shapes=[pltpu.VMEM((n * block, width), bf16)],
        name="encoder_grad",
    )(res_t, *grads, *([so_far] if last else []))


def per_device(residual_rows, encoder, decoder, enc_bias, dec_bias):
    row_count = residual_rows.shape[0]
    loss_scale = 1.0 / math.sqrt(row_count)
    block = row_count // N_SRC
    y, x, core = (lax.axis_index(a) for a in ("y", "xl", "core"))
    ring = lax.axis_index(RING)
    first = core == 0

    def owner_row(offsets, slot):
        rows = []
        for c in range(N_CORE):
            oy, ox = behind(y, x, place(offsets, slot, c))
            rows.append((oy * N_XL + ox) * block)
        return jnp.where(first, rows[0], rows[1])

    def rows_of(start, count):
        return lax.dynamic_slice_in_dim(residual_rows, start, count, 0)

    twin = (NEAR[2],) * 4

    def sum_src(far_parts, near_parts):
        near1, near3, sent, kept = near_parts
        got = [move(part, FAR, slot, True) for slot, part in enumerate(far_parts)]
        got += [move(near1, NEAR, 1, True), move(near3, NEAR, 3, True), move(sent, twin, 0, True)]
        total = kept.astype(f32)
        for part in got:
            total = total + part.astype(f32)
        return total

    def gather_src(shard):
        far = [move(shard, FAR, slot, False) for slot in (3, 2, 1, 0)][::-1]
        near3, near1 = (move(shard, NEAR, slot, False) for slot in (3, 1))
        mate = move(shard, twin, 0, False)
        near = [jnp.where(first, shard, mate), near1, jnp.where(first, mate, shard), near3]
        return near, far

    far_rows = [owner_row(FAR, slot) // block for slot in range(4)]
    near_rows = [owner_row(NEAR, slot) // block for slot in range(4)]
    own_row = (y * N_XL + x) * block
    twin_row = owner_row(twin, 0)
    far_parts = blocks_dot(
        encoder, 0, [bf16] * 4, source=residual_rows, order=jnp.stack(far_rows)
    )
    near_parts = blocks_dot(
        encoder,
        0,
        [bf16, bf16, bf16, f32],
        source=residual_rows,
        order=jnp.stack([near_rows[1], near_rows[3], twin_row // block, own_row // block]),
    )
    pre_act = sum_src(far_parts, near_parts) + enc_bias[None, :]
    latent = (jax.nn.softplus(SHARPNESS * pre_act) / SHARPNESS).astype(bf16)
    slope = jax.nn.sigmoid(SHARPNESS * pre_act)

    near, far = gather_src(latent)

    def core_sum(blocks):
        sent = dot(jnp.concatenate(blocks[2:], axis=0), decoder).astype(bf16)
        theirs = swap(sent, "core", N_CORE, 1)
        mine = dot(jnp.concatenate(blocks[:2], axis=0), decoder) + theirs.astype(f32)
        return mine.astype(bf16), sent

    rows = 4 * block // N_RING
    near_sum, theirs_done = core_sum(near)
    far_blocks = lax.optimization_barrier(tuple(far) + (theirs_done, near[1]))[:4]
    far_sum, _ = core_sum(far_blocks)
    shares = jnp.concatenate([near_sum, far_sum], axis=0)
    weights, shares = lax.optimization_barrier((decoder, shares))
    squares = jnp.sum(jnp.square(weights.astype(f32)), axis=1)
    shares = lax.all_to_all(shares.reshape(N_RING, rows, -1), RING, 0, 0)

    own_sq = squares + swap(squares, "xl", N_XL, 1)
    own_sq = own_sq + swap(own_sq, "y", N_Y, 1)
    other_sq = swap(own_sq, "y", N_Y, 2)
    own_norm = jnp.sqrt(own_sq + EPSILON)
    penalty = PENALTY * (own_norm + jnp.sqrt(other_sq + EPSILON))
    dec_bias, own_norm, penalty = lax.optimization_barrier((dec_bias, own_norm, penalty))

    recon = jnp.broadcast_to(dec_bias[None, :], shares.shape[1:])
    for i in range(N_RING):
        recon = recon + shares[i].astype(f32)
    per_block = N_RING // 4
    starts = jnp.stack([owner_row(o, slot) for o in (NEAR, FAR) for slot in range(2)])
    start = lax.dynamic_index_in_dim(starts, ring // per_block, 0, False)
    target = rows_of(start + (ring % per_block) * rows, rows)
    errors = (recon - target.astype(f32)).astype(bf16)
    order = jnp.stack(near_rows + far_rows)
    order, errors = lax.optimization_barrier((order, errors))
    res_t = transpose(residual_rows, order, block)
    errors = jnp.broadcast_to(errors[None], (N_RING,) + errors.shape)
    mine = lax.all_to_all(errors, RING, 0, 0).reshape(4, block, -1)
    mine, res_t = lax.optimization_barrier((mine, res_t))
    theirs = swap(mine, "core", N_CORE, 1)
    near_err = [mine[0], mine[1], theirs[0], theirs[1]]
    far_err = [mine[2], mine[3], theirs[2], theirs[3]]

    types = [bf16] * 4
    far0, far1, near1, low = blocks_dot(
        decoder, 1, types, blocks=[far_err[0], far_err[1], near_err[1], near_err[0]]
    )
    far2, far3, near3, high = blocks_dot(
        decoder, 1, types, blocks=[far_err[2], far_err[3], near_err[3], near_err[2]]
    )
    sent, kept = jnp.where(first, high, low), jnp.where(first, low, high)
    act_grad = sum_src([far0, far1, far2, far3], [near1, near3, sent, kept]) + penalty[None, :]
    grad_decoder = decoder_grad(
        near + far, near_err + far_err, decoder, jnp.stack([own_norm] * 8), loss_scale
    )
    slope, grad_decoder = lax.optimization_barrier((slope, grad_decoder))
    grad_pre = (loss_scale * act_grad * slope).astype(bf16)
    near_grad, far_grad = gather_src(grad_pre)

    grad_encoder = encoder_grad(res_t, far_grad, 1, None)
    grad_encoder = encoder_grad(res_t, near_grad, 0, grad_encoder)
    return (grad_encoder, grad_decoder)


def solution(mesh):
    fine = Mesh(mesh.devices.reshape(SHAPE), NAMES)
    in_specs = (P(None, SRC), P(SRC, LAT), P(LAT, SRC), P(LAT), P(SRC))
    out_specs = (P(SRC, LAT), P(LAT, SRC))
    return jax.shard_map(
        per_device, mesh=fine, in_specs=in_specs, out_specs=out_specs, check_vma=False
    )
```
